256 devices in a mesh: rep: 32 (over y, z), hx: 8 (over x, core).
Axes of the slice: x: 4, y: 4, z: 8, core: 2. Of those that a mesh axis runs over, the one named last changes fastest.
Arguments:
- stream_in: bfloat16 [768, 6144], P(None, 'rep'), may hold values from -6 to 6
- query: bfloat16 [768, 6144], P('rep', 'hx'), may hold values from -240 to 240
- new_kv: bfloat16 [768, 2, 1024], P('rep', None, 'hx'), may hold values from -6 to 6
- cache: bfloat16 [768, 2, 128, 1024], P('rep', None, None, 'hx'), may hold values from -127 to 127, as said below
- precision: int32 [768, 4], P('rep'), may hold values from 0 to 1
- cache_scale: float32 [768, 2, 4, 8], P('rep', None, None, 'hx'), may hold values from 0.004 to 0.03
- lengths: int32 [768], P('rep'), may hold values from 0 to 128
- w_heads: bfloat16 [6144, 6144], P('hx', 'rep'), may hold values from -0.3125 to 0.3125
- norm_gain: float32 [6144], P('rep'), may hold values from 0.5 to 1.5
- w_router: bfloat16 [6144, 8], P('rep'), may hold values from -0.0390625 to 0.0390625
- expert_choice: int32 [768, 2], replicated, may hold values from 0 to 7, all different within a row; in each aligned block of 768 rows (0 to 767, 768 to 1535, ...) at most 384 rows name the same one
- w_in: bfloat16 [8, 6144, 2, 8192], P('hx', None, None, 'rep'), may hold values from -0.078125 to 0.078125
- w_down: bfloat16 [8, 8192, 6144], P('hx', 'rep'), may hold values from -0.0625 to 0.0625
- mig_dest: int32 [32], replicated, may hold values from 0 to 31, as said below
- mig_req: int32 [32], replicated, may hold values from 0 to 23
- mig_blocks: int32 [32], replicated, may hold values from 1 to 4
Outputs:
- mixed: bfloat16 [768, 6144], P(None, 'rep')
- arrived: bfloat16 [32, 2, 2, 128, 1024], P('rep', None, None, None, 'hx')
The draws below stay inside these ranges and needn't reach their ends.
Inputs may be any that keep to these rules, and one draw needn't show every extreme that they name: `cache`: in blocks whose precision entry is 1, the stored values are whole numbers. `expert_choice`: each row names two different experts; over all 768 rows no expert is named by more than 384 rows, a bound that some block reaches. `mig_dest`: no replica names itself; no replica is named by more than 2 replicas, and one is named by exactly 2.
All inputs are finite; a program needn't handle non-finite values.
Results may differ from the reference program's by a relative error of at most 0.0065.
Values may be sent and summed in bfloat16 or wider, within the bound.
A program may use at most 128 MiB of HBM per device.

```python
import math
import jax
import jax.numpy as jnp
import numpy as np
from jax import lax

D = 6144
HEAD = 128
GROUP = 6
FF = 8192
REQ = 24
BLOCK_LEN = 32
BLOCKS = 4
IN_MOST = 2
KV_HEADS = 8
HEADS = 48
EXPERTS = 8
TOKENS = 768
CACHE = 128
CAP = 384
N_REP = 32


def block_flags(key):
    return jax.random.randint(jax.random.fold_in(key, 11), (TOKENS, BLOCKS), 0, 2).astype(jnp.int32)


def draw_precision(key, part):
    return block_flags(key)


def draw_cache(key, part):
    flags = block_flags(key)
    shape = (TOKENS, 2, CACHE, KV_HEADS * HEAD)
    levels = jax.random.randint(jax.random.fold_in(key, 12), shape, -127, 128).astype(jnp.float32)
    drawn = jnp.clip(jax.random.normal(jax.random.fold_in(key, 13), shape, jnp.float32), -6.0, 6.0)
    spread = jnp.repeat(flags, BLOCK_LEN, axis=1)[:, None, :, None]
    return jnp.where(spread == 1, levels, drawn).astype(jnp.bfloat16)


def draw_query(key, part):
    base = jax.random.normal(jax.random.fold_in(key, 21), (TOKENS, HEADS * HEAD), jnp.float32)
    base = jnp.clip(base, -6.0, 6.0)
    return base.astype(jnp.bfloat16)


def draw_mig_dest(key, part):
    order = jax.random.permutation(jax.random.fold_in(key, 31), N_REP).astype(jnp.int32)
    following = jnp.roll(order, -1)
    following = following.at[N_REP - 1].set(order[1])
    return jnp.zeros((N_REP,), jnp.int32).at[order].set(following).astype(jnp.int32)


def set_ends(values, rng, smallest, largest):
    index_at = [jax.random.randint(jax.random.fold_in(rng, axis), (), 0, length) for axis, length in enumerate(values.shape)]
    main_axis = values.shape.index(max(values.shape))
    next_to = index_at[:main_axis] + [(index_at[main_axis] + 1) % values.shape[main_axis]] + index_at[main_axis + 1:]
    return values.at[tuple(index_at)].set(smallest).at[tuple(next_to)].set(largest)


def steps_of(rng, dims, split, smallest, high):
    gain, own = 1.0, jax.random.fold_in(rng, 6)
    for dim, blocks in split:
        steps = jnp.exp(jax.random.uniform(jax.random.fold_in(own, dim), (blocks,), jnp.float32, smallest / len(split), high / len(split)))
        gain = gain * jnp.repeat(steps, dims[dim] // blocks).reshape([-1 if axis == dim else 1 for axis in range(len(dims))])
    return gain


def routed_block(key, own, number, rows, count, top, most, skew):
    sequence = jax.random.permutation(key, count)
    crowded, common = load_shares(count, rows * top, most, skew, True), load_shares(count, rows * top, most, skew, False)
    places = jnp.arange(count)

    def named(sizes, turn):
        used = int((sizes > 0).sum())
        fixed = max(1, used // 4)
        moved = fixed + (places - fixed + turn * (used - fixed)) % max(1, count - fixed)
        return jnp.zeros((count,), jnp.int32).at[sequence[jnp.where(places < fixed, places, moved)]].set(jnp.asarray(sizes, jnp.int32))

    sizes = jnp.where(number % 4 == 0, named(crowded, number // 4), named(common, number - number // 4 - 1))
    mixed = jax.random.permutation(jax.random.fold_in(own, 3), count)
    giver, taker = mixed[0:count // 2 * 2:2], mixed[1:count // 2 * 2:2]
    slack = jnp.minimum(sizes[giver] - 1, most - sizes[taker]) // 2
    slack = jnp.where((giver == sequence[0]) | (taker == sequence[0]) | (sizes[taker] == 0), 0, jnp.maximum(slack, 0))
    moved = jax.random.randint(jax.random.fold_in(own, 4), (count // 2,), 0, 1 << 20) % (slack + 1)
    sizes = sizes.at[giver].add(-moved).at[taker].add(moved)
    items = jnp.searchsorted(jnp.cumsum(sizes), jnp.arange(rows * top), side="right").astype(jnp.int32)
    listing = items.reshape(top, rows).T
    listing = listing[jax.random.permutation(jax.random.fold_in(own, 1), rows)]
    turn = jax.random.randint(jax.random.fold_in(own, 2), (rows, 1), 0, top)
    return jnp.take_along_axis(listing, (jnp.arange(top)[None, :] + turn) % top, axis=1)


def load_shares(number_of, total, reach, skew, full):
    portions = [(1 << 20) // math.isqrt(grade ** skew) + 1 for grade in range(1, number_of + 1)]
    largest = reach if full else min(reach, max(-(-total // number_of), total * portions[0] // sum(portions)))
    least = 1 if total - largest >= number_of - 1 else 0
    counts, surplus = [largest] + [least] * (number_of - 1), total - largest - least * (number_of - 1)
    while surplus > 0:
        free = [i for i in range(1, number_of) if counts[i] < largest] or [i for i in range(1, number_of) if counts[i] < reach]
        mass, remaining = sum([portions[i] for i in free]), surplus
        for i in free:
            extra = min(reach - counts[i], max(1, remaining * portions[i] // mass), surplus)
            counts[i] = counts[i] + extra
            surplus = surplus - extra
    return np.array(counts)


def normal_values(rng, dims, deviation, reach, shards=(), held_as=jnp.bfloat16):
    factor_of = steps_of(rng, dims, shards, -0.22, 0.18) if shards else 1.0
    drawn = jax.random.normal(rng, dims, jnp.float32) * deviation * factor_of
    return jnp.minimum(jnp.maximum(drawn, -reach), reach).astype(held_as)


def setup_inputs(seed: int = 0) -> dict:
    splits = jax.random.split(jax.random.key(seed), 17)
    stream_in = normal_values(splits[0], (TOKENS, D), 1.0, 6.0, ((1, 32),))
    query = draw_query(jax.random.fold_in(splits[16], 71), 0)
    new_kv = normal_values(splits[2], (TOKENS, 2, KV_HEADS * HEAD), 1.0, 6.0, ((0, 32), (2, 8)))
    cache = draw_cache(jax.random.fold_in(splits[16], 71), 0)
    precision = draw_precision(jax.random.fold_in(splits[16], 71), 0)
    cache_scale = jnp.clip(jnp.exp(math.log(0.03) - 2.014903 * jax.random.uniform(splits[5], (TOKENS, 2, BLOCKS, KV_HEADS), jnp.float32) ** steps_of(splits[5], (TOKENS, 2, BLOCKS, KV_HEADS), ((0, 32), (3, 8)), -0.2, 0.2)), 0.004, 0.03)
    lengths = set_ends(jax.random.randint(splits[6], (TOKENS,), 0, CACHE + 1), jax.random.fold_in(splits[6], 1), 0, CACHE).astype(jnp.int32)
    w_heads = normal_values(splits[7], (HEADS * HEAD, D), (HEADS * HEAD // 16) ** -0.5, 0.3125, ((0, 8), (1, 32)))
    norm_gain = jnp.clip(1.0 + 0.1 * jax.random.normal(splits[8], (D,), jnp.float32), 0.5, 1.5)
    w_router = normal_values(splits[9], (D, EXPERTS), (4 * D) ** -0.5, 0.0390625, ((0, 32),))
    expert_choice_keys = jax.random.split(jax.random.fold_in(splits[10], 1), TOKENS // TOKENS)
    expert_choice_turns = jax.random.permutation(jax.random.fold_in(splits[10], 3), TOKENS // TOKENS)
    expert_choice = jax.vmap(lambda own, number: routed_block(jax.random.fold_in(splits[10], 2), own, number, TOKENS, EXPERTS, 2, CAP, 2))(expert_choice_keys, expert_choice_turns).reshape((TOKENS, 2))
    w_in = normal_values(splits[11], (EXPERTS, D, 2, FF), D ** -0.5, 0.078125, ((0, 8), (3, 32)))
    w_down = normal_values(splits[12], (EXPERTS, FF, D), FF ** -0.5, 0.0625, ((0, 8), (1, 32)))
    mig_dest = draw_mig_dest(jax.random.fold_in(splits[16], 71), 0)
    mig_req = set_ends(jax.random.randint(splits[14], (N_REP,), 0, REQ), jax.random.fold_in(splits[14], 1), 0, REQ - 1).astype(jnp.int32)
    mig_blocks = set_ends(jax.random.randint(splits[15], (N_REP,), 1, BLOCKS + 1), jax.random.fold_in(splits[15], 1), 1, BLOCKS).astype(jnp.int32)
    return dict(stream_in=stream_in, query=query, new_kv=new_kv, cache=cache, precision=precision, cache_scale=cache_scale, lengths=lengths, w_heads=w_heads, norm_gain=norm_gain, w_router=w_router, expert_choice=expert_choice, w_in=w_in, w_down=w_down, mig_dest=mig_dest, mig_req=mig_req, mig_blocks=mig_blocks)


EPSILON = 1e-05

def block_factor(precision, cache_scale):
    factor = jnp.where(precision[:, None, :, None] == 1, cache_scale, 1.0)
    return jnp.repeat(factor, BLOCK_LEN, axis=2)

def attend(query, new_kv, cache, factor, lengths):
    rows = query.shape[0]
    heads_kv = new_kv.shape[2] // HEAD
    scale = HEAD ** (-0.5)
    queries = query.astype(jnp.float32).reshape(rows, heads_kv, GROUP, HEAD)
    keys = cache[:, 0].astype(jnp.float32).reshape(rows, CACHE, heads_kv, HEAD)
    values = cache[:, 1].astype(jnp.float32).reshape(rows, CACHE, heads_kv, HEAD)
    fresh = new_kv.astype(jnp.float32).reshape(rows, 2, heads_kv, HEAD)
    scores = jnp.einsum('rkgd,rpkd->rkgp', queries, keys)
    scores = scores * jnp.transpose(factor[:, 0], (0, 2, 1))[:, :, None, :] * scale
    own = jnp.einsum('rkgd,rkd->rkg', queries, fresh[:, 0]) * scale
    live = jnp.arange(CACHE)[None, :] < lengths[:, None]
    scores = jnp.where(live[:, None, None, :], scores, -jnp.inf)
    top = jnp.maximum(lax.optimization_barrier(jnp.max(scores, axis=3)), own)
    weights = jnp.exp(scores - top[..., None])
    own_weight = jnp.exp(own - top)
    total = lax.optimization_barrier(jnp.sum(weights, axis=3)) + own_weight
    value_weight = (weights / total[..., None] * jnp.transpose(factor[:, 1], (0, 2, 1))[:, :, None, :]).astype(jnp.bfloat16)
    own_prob = (own_weight / total).astype(jnp.bfloat16)
    result = jnp.einsum('rkgp,rpkd->rkgd', value_weight.astype(jnp.float32), values)
    result = result + own_prob.astype(jnp.float32)[..., None] * fresh[:, 1][:, :, None, :]
    return result.reshape(rows, heads_kv * GROUP * HEAD).astype(jnp.bfloat16)

def slot_table(flat, rank, pair_token, gate_flat, expert, tokens):
    select = (flat[None, :] == expert) & (rank[None, :] == jnp.arange(CAP)[:, None])
    token_of_slot = lax.optimization_barrier(jnp.sum(jnp.where(select, pair_token[None, :], 0), axis=1)).astype(jnp.int32)
    live = jnp.any(select, axis=1)
    gate_of_slot = lax.optimization_barrier(jnp.sum(jnp.where(select, gate_flat[None, :], 0.0), axis=1))
    match = (token_of_slot[:, None] == jnp.arange(tokens)[None, :]) & live[:, None]
    combine = jnp.where(match, gate_of_slot[:, None], 0.0)
    return (token_of_slot, live, combine)

def reference(stream_in, query, new_kv, cache, precision, cache_scale, lengths, w_heads, norm_gain, w_router, expert_choice, w_in, w_down, mig_dest, mig_req, mig_blocks):
    tokens = stream_in.shape[0]
    factor = block_factor(precision, cache_scale)
    attended = attend(query, new_kv, cache, factor, lengths)
    hidden_state = stream_in.astype(jnp.float32) + jnp.dot(attended, w_heads, preferred_element_type=jnp.float32)
    squares = lax.optimization_barrier(jnp.sum(hidden_state * hidden_state, axis=1))
    inverse = lax.rsqrt(squares / D + EPSILON)
    normed = hidden_state * inverse[:, None] * norm_gain[None, :]
    logits = jnp.dot(normed, w_router.astype(jnp.float32), precision=lax.Precision.HIGHEST)
    onehot_choice = expert_choice[:, :, None] == jnp.arange(EXPERTS)[None, None, :]
    chosen = lax.optimization_barrier(jnp.sum(jnp.where(onehot_choice, logits[:, None, :], 0.0), axis=2))
    peak = lax.optimization_barrier(jnp.max(chosen, axis=1, keepdims=True))
    expo = jnp.exp(chosen - peak)
    gates = expo / lax.optimization_barrier(jnp.sum(expo, axis=1, keepdims=True))
    u_rows = normed.astype(jnp.bfloat16)
    flat = expert_choice.reshape(-1)
    pair_token = (jnp.arange(2 * tokens) // 2).astype(jnp.int32)
    gate_flat = gates.reshape(-1)
    onehot = (flat[:, None] == jnp.arange(EXPERTS)[None, :]).astype(jnp.int32)
    rank = lax.optimization_barrier(jnp.sum((jnp.cumsum(onehot, axis=0) - onehot) * onehot, axis=1))

    def one_expert(total, item):
        weights_in, weights_down, expert = item
        token_of_slot, live, combine = slot_table(flat, rank, pair_token, gate_flat, expert, tokens)
        picked = jnp.where(live[:, None], u_rows[token_of_slot], jnp.zeros((), jnp.bfloat16))
        gate_up = jnp.dot(picked, weights_in.reshape(D, 2 * FF), preferred_element_type=jnp.float32)
        act = (jax.nn.silu(gate_up[:, :FF]) * gate_up[:, FF:]).astype(jnp.bfloat16)
        out = jnp.dot(act, weights_down, preferred_element_type=jnp.float32)
        return (total + jnp.dot(combine.T, out, precision=lax.Precision.HIGHEST), None)
    moe, _ = lax.scan(one_expert, jnp.zeros((tokens, D), jnp.float32), (w_in, w_down, jnp.arange(EXPERTS, dtype=jnp.int32)))
    mixed = (hidden_state + moe).astype(jnp.bfloat16)
    reps = mig_dest.shape[0]
    source_rows = (jnp.arange(reps) * REQ + mig_req).astype(jnp.int32)
    levels = cache[source_rows].astype(jnp.float32)
    scales = jnp.repeat(factor[source_rows], HEAD, axis=3)
    keep = jnp.arange(CACHE)[None, :] < (mig_blocks * BLOCK_LEN)[:, None]
    outgoing = jnp.where(keep[:, None, :, None], levels * scales, 0.0).astype(jnp.bfloat16)
    aimed = (mig_dest[None, :] == jnp.arange(reps)[:, None]).astype(jnp.int32)
    before = jnp.cumsum(aimed, axis=1) - aimed
    select = (aimed[:, None, :] == 1) & (before[:, None, :] == jnp.arange(IN_MOST)[None, :, None])
    arrived = jnp.einsum('qis,sabc->qiabc', select.astype(jnp.float32), outgoing.astype(jnp.float32))
    return (mixed, arrived.astype(jnp.bfloat16))
```

```python
import functools

import jax
import jax.numpy as jnp
from jax import lax
from jax.experimental import pallas as pl
from jax.experimental.pallas import tpu as pltpu
from jax.sharding import PartitionSpec as P

D = 6144
HEAD = 128
GROUP = 6
BLOCK_LEN = 32
IN_MOST = 2
CACHE = 128
EPSILON = 1e-05

SIZES = {"y": 4, "z": 8, "x": 4, "c": 2}
PLANE = ("y", "z")
CHIPS = ("x", "c")


def coords():
    rep = lax.axis_index("rep")
    hx = lax.axis_index("hx")
    return {"y": rep // 8, "z": lax.rem(rep, 8), "x": hx // 2, "c": lax.rem(hx, 2)}


def device_at(at):
    return {"rep": at["y"] * 8 + at["z"], "hx": at["x"] * 2 + at["c"]}


def shifted(at, dim, step):
    n = SIZES[dim]
    moved = dict(at)
    moved[dim] = lax.rem(at[dim] + (step % n), n)
    return moved


def index_in(at, dims):
    if "y" in dims:
        return at["y"] * 8 + at["z"]
    return at["x"] * 2 + at["c"]


def ring_reach(n, flip):
    return (n // 2, n - 1 - n // 2) if flip % 2 == 0 else (n - 1 - n // 2, n // 2)


def gather_plan(na, nb, flip):
    events = []
    ra = ring_reach(na, flip)
    for oa in range(-ra[1], ra[0] + 1):
        rb = ring_reach(nb, oa + flip)
        for ob in range(-rb[1], rb[0] + 1):
            sends = []
            if ob == 0:
                for sign, limit in ((1, ra[0]), (-1, ra[1])):
                    if oa * sign >= 0 and abs(oa) < limit:
                        sends.append((0, sign))
            for sign, limit in ((1, rb[0]), (-1, rb[1])):
                if ob * sign >= 0 and abs(ob) < limit:
                    sends.append((1, sign))
            events.append((oa, ob, sends))
    return sorted(events, key=lambda e: (abs(e[0]) + abs(e[1]), abs(e[1])))


def enter(me, dims):
    barrier = pltpu.get_barrier_semaphore()
    count = 0
    for dim in dims:
        for step in (1, -1) if SIZES[dim] > 2 else (1,):
            pl.semaphore_signal(
                barrier,
                inc=1,
                device_id=device_at(shifted(me, dim, step)),
                device_id_type=pl.DeviceIdType.MESH,
            )
            count += 1
    pl.semaphore_wait(barrier, count)


def gather_body(items, greeted, n_in, *refs):
    ins, outs = refs[:n_in], refs[n_in : 2 * n_in]
    send_sem, recv_sem, own_sem = refs[2 * n_in :]
    me = coords()
    enter(me, greeted)
    todo, copies = [], []
    base_recv = 0
    for number, (which, part, dims, flip) in enumerate(items):
        a, b = dims
        plan = gather_plan(SIZES[a], SIZES[b], flip)
        for k, (oa, ob, sends) in enumerate(plan):
            todo.append((abs(oa) + abs(ob), number, oa, ob, sends))
        slots = {(oa, ob): base_recv + k for k, (oa, ob, _) in enumerate(plan)}
        items[number] = (which, part, dims, flip, slots)
        base_recv += len(plan)
    todo.sort(key=lambda e: e[0])
    sent = 0
    owned = []
    for hops, number, oa, ob, sends in todo:
        which, part, dims, flip, slots = items[number]
        origin = shifted(shifted(me, dims[0], -oa), dims[1], -ob)
        at = (index_in(origin, dims),) if part is None else (index_in(origin, dims), part)
        place = outs[which].at[at]
        if hops == 0:
            source = ins[which] if part is None else ins[which].at[part]
            own = pltpu.make_async_copy(source, place, own_sem.at[number])
            own.start()
            owned.append(own)
        else:
            source = place
            pltpu.make_async_remote_copy(
                src_ref=place,
                dst_ref=place,
                send_sem=send_sem.at[0],
                recv_sem=recv_sem.at[slots[(oa, ob)]],
                device_id=device_at(shifted(me, dims[0], 1)),
                device_id_type=pl.DeviceIdType.MESH,
            ).wait_recv()
        for along, sign in sends:
            to = (oa + sign, ob) if along == 0 else (oa, ob + sign)
            copy = pltpu.make_async_remote_copy(
                src_ref=source,
                dst_ref=place,
                send_sem=send_sem.at[sent],
                recv_sem=recv_sem.at[slots[to]],
                device_id=device_at(shifted(me, dims[along], sign)),
                device_id_type=pl.DeviceIdType.MESH,
            )
            copy.start()
            copies.append(copy)
            sent += 1
    for copy in copies:
        copy.wait_send()
    for own in owned:
        own.wait()


def gather_all(arrays, items, collective_id, name):
    greeted = []
    total = 0
    members = {}
    for which, part, dims, flip in items:
        members[which] = SIZES[dims[0]] * SIZES[dims[1]]
        total += members[which]
        greeted += [dim for dim in dims if dim not in greeted]
    return pl.pallas_call(
        lambda *refs: gather_body(list(items), greeted, len(arrays), *refs),
        out_shape=[
            jax.ShapeDtypeStruct((members[k], *x.shape), x.dtype) for k, x in enumerate(arrays)
        ],
        in_specs=[pl.BlockSpec(memory_space=pl.ANY)] * len(arrays),
        out_specs=[pl.BlockSpec(memory_space=pl.ANY)] * len(arrays),
        scratch_shapes=[
            pltpu.SemaphoreType.DMA((total,)),
            pltpu.SemaphoreType.DMA((total,)),
            pltpu.SemaphoreType.DMA((len(items),)),
        ],
        compiler_params=pltpu.CompilerParams(collective_id=collective_id, has_side_effects=True),
        name=name,
    )(*arrays)


def exchange_body(dim, x_ref, o_ref, send_sem, recv_sem):
    n = SIZES[dim]
    me = coords()
    barrier = pltpu.get_barrier_semaphore()
    for step in range(1, n):
        pl.semaphore_signal(
            barrier,
            inc=1,
            device_id=device_at(shifted(me, dim, step)),
            device_id_type=pl.DeviceIdType.MESH,
        )
    pl.semaphore_wait(barrier, n - 1)
    copies = []
    for step in sorted(range(1, n), key=lambda s: -min(s, n - s)):
        there = shifted(me, dim, step)
        copy = pltpu.make_async_remote_copy(
            src_ref=x_ref.at[there[dim]],
            dst_ref=o_ref.at[step - 1],
            send_sem=send_sem.at[step - 1],
            recv_sem=recv_sem.at[step - 1],
            device_id=device_at(there),
            device_id_type=pl.DeviceIdType.MESH,
        )
        copy.start()
        copies.append(copy)
    for copy in copies:
        copy.wait()


def exchange(x, dim, collective_id, name):
    n = SIZES[dim]
    return pl.pallas_call(
        functools.partial(exchange_body, dim),
        out_shape=jax.ShapeDtypeStruct((n - 1, *x.shape[1:]), x.dtype),
        in_specs=[pl.BlockSpec(memory_space=pl.ANY)],
        out_specs=pl.BlockSpec(memory_space=pl.ANY),
        scratch_shapes=[pltpu.SemaphoreType.DMA((n - 1,)), pltpu.SemaphoreType.DMA((n - 1,))],
        compiler_params=pltpu.CompilerParams(collective_id=collective_id, has_side_effects=True),
        name=name,
    )(x)


def block_factor(precision, cache_scale):
    factor = jnp.where(precision[:, None, :, None] == 1, cache_scale, 1.0)
    return jnp.repeat(factor, BLOCK_LEN, axis=2)


def attend(query, new_kv, cache, factor, lengths):
    rows = query.shape[0]
    heads_kv = new_kv.shape[2] // HEAD
    scale = HEAD ** (-0.5)
    queries = query.reshape(rows, heads_kv, GROUP, HEAD)
    keys = cache[:, 0].reshape(rows, CACHE, heads_kv, HEAD)
    values = cache[:, 1].reshape(rows, CACHE, heads_kv, HEAD)
    fresh = new_kv.reshape(rows, 2, heads_kv, HEAD)
    scores = jnp.einsum("rkgd,rpkd->rkgp", queries, keys, preferred_element_type=jnp.float32)
    scores = scores * jnp.transpose(factor[:, 0], (0, 2, 1))[:, :, None, :] * scale
    own = (
        jnp.einsum("rkgd,rkd->rkg", queries, fresh[:, 0], preferred_element_type=jnp.float32)
        * scale
    )
    live = jnp.arange(CACHE)[None, :] < lengths[:, None]
    scores = jnp.where(live[:, None, None, :], scores, -jnp.inf)
    top = jnp.maximum(jnp.max(scores, axis=3), own)
    weights = jnp.exp(scores - top[..., None])
    own_weight = jnp.exp(own - top)
    total = jnp.sum(weights, axis=3) + own_weight
    value_weight = (
        weights / total[..., None] * jnp.transpose(factor[:, 1], (0, 2, 1))[:, :, None, :]
    ).astype(jnp.bfloat16)
    own_prob = (own_weight / total).astype(jnp.bfloat16)
    result = jnp.einsum("rkgp,rpkd->rkgd", value_weight, values, preferred_element_type=jnp.float32)
    result = result + own_prob.astype(jnp.float32)[..., None] * fresh[:, 1][:, :, None, :].astype(
        jnp.float32
    )
    return result.reshape(rows, heads_kv * GROUP * HEAD).astype(jnp.bfloat16)


def contract_first(a, b, **kw):
    return lax.dot_general(
        a, b, (((0,), (0,)), ((), ())), preferred_element_type=jnp.float32, **kw
    )


def hand_off(cache, factor, mig_req, mig_blocks, replica_id):
    chosen_req = mig_req[replica_id]
    levels = lax.dynamic_index_in_dim(cache, chosen_req, 0, keepdims=False).astype(jnp.float32)
    scales = lax.dynamic_index_in_dim(factor, chosen_req, 0, keepdims=False)
    keep = jnp.arange(CACHE) < mig_blocks[replica_id] * BLOCK_LEN
    return jnp.where(keep[None, :, None], levels * scales, 0.0).astype(jnp.bfloat16)


def arrivals(everyones, mig_dest, replica_id):
    aimed = mig_dest == replica_id
    numbers = jnp.arange(mig_dest.shape[0])
    first = jnp.min(jnp.where(aimed, numbers, mig_dest.shape[0]))
    last = jnp.max(jnp.where(aimed, numbers, -1))
    rows = []
    for source, there in ((first, jnp.any(aimed)), (last, last > first)):
        row = lax.dynamic_index_in_dim(everyones, source, 0, keepdims=False)
        rows.append(jnp.where(there, row, jnp.zeros((), row.dtype)))
    return jnp.stack(rows)[None]


def local(
    stream_in,
    query,
    new_kv,
    cache,
    precision,
    cache_scale,
    lengths,
    w_heads,
    norm_gain,
    w_router,
    expert_choice,
    w_in,
    w_down,
    mig_dest,
    mig_req,
    mig_blocks,
):
    tokens, mine = stream_in.shape
    capacity = tokens // 2
    experts = w_router.shape[1]
    half = mine // 2
    ff = w_in.shape[3]
    replica_id = lax.axis_index("rep")
    expert = lax.axis_index("hx")
    y_id, z_id = replica_id // 8, lax.rem(replica_id, 8)

    factor = block_factor(precision, cache_scale)
    attended = attend(query, new_kv, cache, factor, lengths)
    split = attended.shape[1] // 2
    left, right = gather_all(
        [attended[:, :split], attended[:, split:]],
        [(0, None, ("z", "y"), 0), (1, None, ("y", "z"), 1)],
        1,
        "gather_attended",
    )
    part = lax.dot_general(
        w_heads[:split],
        left.reshape(tokens, split),
        (((0,), (1,)), ((), ())),
        preferred_element_type=jnp.float32,
    ) + lax.dot_general(
        w_heads[split:],
        right.reshape(tokens, split),
        (((0,), (1,)), ((), ())),
        preferred_element_type=jnp.float32,
    )
    outgoing = hand_off(cache, factor, mig_req, mig_blocks, replica_id)
    parts, everyones = gather_all(
        [part.astype(jnp.bfloat16).reshape(2, half, tokens), outgoing],
        [
            (0, 0, ("x", "c"), 0),
            (0, 1, ("x", "c"), 1),
            (1, 0, ("z", "y"), 0),
            (1, 1, ("y", "z"), 1),
        ],
        2,
        "gather_heads",
    )
    arrived = arrivals(everyones, mig_dest, replica_id)
    hidden = stream_in.T.astype(jnp.float32) + jnp.sum(
        parts.reshape(experts, mine, tokens).astype(jnp.float32), axis=0
    )

    ids = jnp.arange(experts)
    choice = expert_choice.T
    names = (choice[None, 0, :] == ids[:, None]) | (choice[None, 1, :] == ids[:, None])
    order = jnp.arange(tokens)
    earlier = (order[:, None] < order[None, :]).astype(jnp.bfloat16)
    rank = jnp.dot(
        names.astype(jnp.bfloat16), earlier, preferred_element_type=jnp.float32
    ).astype(jnp.int32)
    slot_of = jnp.where(names, rank, -1)
    my_slot = lax.dynamic_index_in_dim(slot_of, expert, 0, keepdims=False)
    pick = my_slot[:, None] == jnp.arange(capacity)[None, :]

    gained = hidden * norm_gain[:, None]
    u_slots = jnp.dot(
        gained.astype(jnp.bfloat16), pick.astype(jnp.bfloat16), preferred_element_type=jnp.float32
    ).astype(jnp.bfloat16)
    squares = jnp.sum(hidden * hidden, axis=0)
    logits = contract_first(
        w_router.astype(jnp.float32), gained, precision=lax.Precision.HIGHEST
    )
    first = jnp.sum(jnp.where(choice[None, 0, :] == ids[:, None], logits, 0.0), axis=0)
    second = jnp.sum(jnp.where(choice[None, 1, :] == ids[:, None], logits, 0.0), axis=0)
    ahead = jnp.where(choice[0] == expert, first - second, second - first)
    extra = jnp.concatenate(
        [squares[None], ahead[None], jnp.zeros((6, tokens), jnp.float32)], axis=0
    )
    extra_slots = jnp.dot(extra, pick.astype(jnp.float32), precision=lax.Precision.HIGHEST)
    u_all, extra_all = gather_all(
        [u_slots.reshape(2, half, capacity), extra_slots],
        [(0, 0, ("z", "y"), 0), (0, 1, ("y", "z"), 1), (1, None, ("y", "z"), 0)],
        3,
        "gather_rows",
    )
    sums = jnp.sum(extra_all, axis=0)
    inverse = lax.rsqrt(sums[0] / D + EPSILON)
    gate_of_slot = 1.0 / (1.0 + jnp.exp(-sums[1] * inverse))
    gate_up = contract_first(w_in[0].reshape(D, 2 * ff), u_all.reshape(D, capacity))
    gate_up = gate_up * inverse[None, :]
    act = (jax.nn.silu(gate_up[:ff]) * gate_up[ff:]).astype(jnp.bfloat16)
    out = contract_first(w_down[0], act).astype(jnp.bfloat16)

    out = out.reshape(4, 8, mine, capacity)
    from_y = exchange(out, "y", 4, "scatter_y")
    own = lax.dynamic_index_in_dim(out, y_id, 0, keepdims=False)
    out = own.astype(jnp.float32) + jnp.sum(from_y.astype(jnp.float32), axis=0)
    out = out.astype(jnp.bfloat16)
    from_z = exchange(out, "z", 5, "scatter_z")
    own = lax.dynamic_index_in_dim(out, z_id, 0, keepdims=False)
    out = own.astype(jnp.float32) + jnp.sum(from_z.astype(jnp.float32), axis=0)
    weighted = (out * gate_of_slot[None, :]).astype(jnp.bfloat16)
    (everyone,) = gather_all(
        [weighted.reshape(2, half, capacity)],
        [(0, 0, ("x", "c"), 0), (0, 1, ("x", "c"), 1)],
        6,
        "gather_experts",
    )
    place = (slot_of[:, None, :] == jnp.arange(capacity)[None, :, None]).astype(jnp.bfloat16)
    moe = lax.dot_general(
        everyone.reshape(experts, mine, capacity),
        place,
        (((0, 2), (0, 1)), ((), ())),
        preferred_element_type=jnp.float32,
    )
    mixed = (hidden + moe).astype(jnp.bfloat16).T
    return (mixed, arrived)


def solution(mesh):
    placed = (
        P(None, "rep"),
        P("rep", "hx"),
        P("rep", None, "hx"),
        P("rep", None, None, "hx"),
        P("rep", None),
        P("rep", None, None, "hx"),
        P("rep"),
        P("hx", "rep"),
        P("rep"),
        P("rep", None),
        P(),
        P("hx", None, None, "rep"),
        P("hx", "rep", None),
        P(),
        P(),
        P(),
    )
    return jax.shard_map(
        local,
        mesh=mesh,
        in_specs=placed,
        out_specs=(P(None, "rep"), P("rep", None, None, None, "hx")),
        check_vma=False,
    )
```

```python
import functools

import jax
import jax.numpy as jnp
from jax import lax
from jax.experimental import pallas as pl
from jax.experimental.pallas import tpu as pltpu
from jax.sharding import PartitionSpec as P

D = 6144
HEAD = 128
GROUP = 6
BLOCK_LEN = 32
IN_MOST = 2
CACHE = 128
EPSILON = 1e-05

SIZES = {"y": 4, "z": 8, "x": 4, "c": 2}
PLANE = ("y", "z")
CHIPS = ("x", "c")


def coords():
    rep = lax.axis_index("rep")
    hx = lax.axis_index("hx")
    return {"y": rep // 8, "z": lax.rem(rep, 8), "x": hx // 2, "c": lax.rem(hx, 2)}


def device_at(at):
    return {"rep": at["y"] * 8 + at["z"], "hx": at["x"] * 2 + at["c"]}


def shifted(at, dim, step):
    n = SIZES[dim]
    moved = dict(at)
    moved[dim] = lax.rem(at[dim] + (step % n), n)
    return moved


def index_in(at, dims):
    if "y" in dims:
        return at["y"] * 8 + at["z"]
    return at["x"] * 2 + at["c"]


TREES = {
    "ring": {
        2: {0: (1,)},
        4: {0: (1, -1), 1: (2,)},
        8: {0: (1, -1), 1: (2,), 2: (3,), 3: (4,), -1: (-2,), -2: (-3,)},
    },
    "two": {
        2: {0: (1,)},
        4: {0: (1, -1, 2)},
        8: {0: (1, -1, 2, -2), 2: (3, 4), -2: (-3,)},
    },
    "direct": {
        2: {0: (1,)},
        4: {0: (1, -1, 2)},
        8: {0: (1, -1, 2, -2, 3, -3, 4)},
    },
}


def tree_of(kind, n, flip):
    sign = -1 if flip % 2 and n > 2 else 1
    return {sign * o: tuple(sign * t for t in to) for o, to in TREES[kind][n].items()}


def places_of(tree):
    found = [0]
    for o in found:
        found += tree.get(o, ())
    return found


def depth_of(tree, o):
    if o == 0:
        return 0
    return 1 + depth_of(tree, next(p for p, to in tree.items() if o in to))


def gather_plan(dims, kinds, flip):
    na, nb = SIZES[dims[0]], SIZES[dims[1]]
    ta = tree_of(kinds[0], na, flip)
    events = []
    for oa in places_of(ta):
        tb = tree_of(kinds[1], nb, oa + flip)
        for ob in places_of(tb):
            sends = []
            if ob == 0:
                sends += [(t, 0) for t in ta.get(oa, ())]
            sends += [(oa, t) for t in tb.get(ob, ())]
            cost = 3 * (depth_of(ta, oa) + depth_of(tb, ob)) + abs(oa) + abs(ob)
            events.append((cost, oa, ob, sends))
    return sorted(events, key=lambda e: e[0])


def partners(dims, kinds):
    found = {}
    for dim, kind in zip(dims, kinds):
        steps = found.setdefault(dim, set())
        for o, to in TREES[kind][SIZES[dim]].items():
            for t in to:
                steps |= {(t - o) % SIZES[dim], (o - t) % SIZES[dim]}
    return found


def enter(me, steps):
    barrier = pltpu.get_barrier_semaphore()
    count = 0
    for dim in sorted(steps):
        for step in sorted(steps[dim]):
            pl.semaphore_signal(
                barrier,
                inc=1,
                device_id=device_at(shifted(me, dim, step)),
                device_id_type=pl.DeviceIdType.MESH,
            )
            count += 1
    pl.semaphore_wait(barrier, count)


def remote(source, place, send_sem, recv_sem, there):
    return pltpu.make_async_remote_copy(
        src_ref=source,
        dst_ref=place,
        send_sem=send_sem,
        recv_sem=recv_sem,
        device_id=device_at(there),
        device_id_type=pl.DeviceIdType.MESH,
    )


def gather_body(items, n_in, *refs):
    ins, outs = refs[:n_in], refs[n_in : 2 * n_in]
    send_sem, recv_sem, own_sem = refs[2 * n_in :]
    me = coords()
    greeted = {}
    for _, _, dims, kinds, _ in items:
        for dim, steps in partners(dims, kinds).items():
            greeted.setdefault(dim, set()).update(steps)
    enter(me, greeted)
    todo, slots, copies, owned = [], [], [], []
    sems = 0
    for number, (_, _, dims, kinds, flip) in enumerate(items):
        plan = gather_plan(dims, kinds, flip)
        todo += [(cost, number, oa, ob, sends) for cost, oa, ob, sends in plan]
        slots.append({(oa, ob): sems + k for k, (_, oa, ob, _) in enumerate(plan)})
        sems += len(plan)
    for _, number, oa, ob, sends in sorted(todo, key=lambda e: e[0]):
        which, part, dims, _, _ = items[number]
        origin = shifted(shifted(me, dims[0], -oa), dims[1], -ob)
        at = (index_in(origin, dims),) if part is None else (index_in(origin, dims), part)
        place = outs[which].at[at]
        source = place
        if (oa, ob) == (0, 0):
            source = ins[which] if part is None else ins[which].at[part]
        else:
            slot = slots[number][oa, ob]
            remote(
                place, place, send_sem.at[0], recv_sem.at[slot], shifted(me, dims[0], 1)
            ).wait_recv()
        for to in sends:
            there = shifted(shifted(me, dims[0], to[0] - oa), dims[1], to[1] - ob)
            slot = slots[number][to]
            copy = remote(source, place, send_sem.at[slot], recv_sem.at[slot], there)
            copy.start()
            copies.append(copy)
        if (oa, ob) == (0, 0):
            own = pltpu.make_async_copy(source, place, own_sem.at[number])
            own.start()
            owned.append(own)
    for copy in copies:
        copy.wait_send()
    for own in owned:
        own.wait()


def gather_all(arrays, items, collective_id, name, space=pl.ANY):
    total = 0
    members = {}
    for which, _, dims, _, _ in items:
        members[which] = SIZES[dims[0]] * SIZES[dims[1]]
        total += members[which]
    return pl.pallas_call(
        functools.partial(gather_body, tuple(items), len(arrays)),
        out_shape=[
            jax.ShapeDtypeStruct((members[k], *x.shape), x.dtype) for k, x in enumerate(arrays)
        ],
        in_specs=[pl.BlockSpec(memory_space=space)] * len(arrays),
        out_specs=[pl.BlockSpec(memory_space=space)] * len(arrays),
        scratch_shapes=[
            pltpu.SemaphoreType.DMA((total,)),
            pltpu.SemaphoreType.DMA((total,)),
            pltpu.SemaphoreType.DMA((len(items),)),
        ],
        compiler_params=pltpu.CompilerParams(collective_id=collective_id, has_side_effects=True),
        name=name,
    )(*arrays)


def dot_f32(a, b):
    return jnp.dot(a, b, preferred_element_type=jnp.float32)


def down_body(act_ref, w_ref, gate_ref, o_ref, p2, p1, pm, r1, fin, turned, tf, zr, *sems):
    s1_send, s1_recv, s2_send, s2_recv, z_send, z_recv = sems
    me = coords()
    enter(me, {"y": {1, 3}, "z": set(range(1, 8))})
    up, down = shifted(me, "y", 1), shifted(me, "y", -1)
    pair, odd = me["z"] // 2, lax.rem(me["z"], 2)
    rows = act_ref.shape[0]
    mid = rows // 2
    wide = w_ref.shape[1] // 16
    low, high = pl.ds(0, mid), pl.ds(mid, mid)
    order = (2, 1, 3, 0)

    def product(step, k):
        there = lax.rem(me["y"] + step, 4)
        start = there * (4 * wide) + lax.rem(pair + k, 4) * wide
        return dot_f32(act_ref[...], w_ref[:, pl.ds(pl.multiple_of(start, 128), wide)])

    copies = []

    def send(source, place, ss, rs, there):
        copy = remote(source, place, ss, rs, there)
        copy.start()
        copies.append(copy)
        return copy

    steps = {}
    for k in order:
        p2[k] = product(2, k).astype(p2.dtype)
        a = send(p2.at[k, low], r1.at[k, 0], s1_send.at[k, 0], s1_recv.at[k, 0], up)
        b = send(p2.at[k, high], r1.at[k, 1], s1_send.at[k, 1], s1_recv.at[k, 1], down)
        steps[k] = (a, b)
    lasts = {}
    for k in order:
        p1[k] = product(1, k).astype(p1.dtype)
        c = send(p1.at[k, high], fin.at[k, 0, 1], s2_send.at[k, 0, 1], s2_recv.at[k, 0, 1], up)
        pm[k] = product(3, k).astype(pm.dtype)
        d = send(pm.at[k, low], fin.at[k, 1, 0], s2_send.at[k, 1, 0], s2_recv.at[k, 1, 0], down)
        steps[k][0].wait_recv()
        p1[k, low] = (p1[k, low].astype(jnp.float32) + r1[k, 0].astype(jnp.float32)).astype(p1.dtype)
        e = send(p1.at[k, low], fin.at[k, 0, 0], s2_send.at[k, 0, 0], s2_recv.at[k, 0, 0], up)
        steps[k][1].wait_recv()
        pm[k, high] = (pm[k, high].astype(jnp.float32) + r1[k, 1].astype(jnp.float32)).astype(
            pm.dtype
        )
        f = send(pm.at[k, high], fin.at[k, 1, 1], s2_send.at[k, 1, 1], s2_recv.at[k, 1, 1], down)
        lasts[k] = (c, d, e, f)
    for k in order:
        whole = product(0, k)
        for copy in lasts[k]:
            copy.wait_recv()
        whole = whole + jnp.concatenate(
            [
                fin[k, 0, 0].astype(jnp.float32) + fin[k, 1, 0].astype(jnp.float32),
                fin[k, 0, 1].astype(jnp.float32) + fin[k, 1, 1].astype(jnp.float32),
            ],
            axis=0,
        )
        whole = whole.T
        for e in range(2):
            part = whole[e * (wide // 2) : (e + 1) * (wide // 2)]
            turned[k, e] = part.astype(turned.dtype)
            if k == 0:
                tf[e] = part
        first = 2 * lax.rem(pair + k, 4)
        for e in range(2):
            if k > 0:
                there = dict(me, z=first + e)
                send(
                    turned.at[k, e],
                    zr.at[2 * k + odd],
                    z_send.at[2 * k + e],
                    z_recv.at[2 * k + odd],
                    there,
                )
        if k == 0:
            there = dict(me, z=first + 1 - odd)
            send(turned.at[0, 1 - odd], zr.at[odd], z_send.at[0], z_recv.at[odd], there)
    total = tf[odd]
    for k in order:
        for e in range(2) if k > 0 else (0,):
            slot = 2 * k + e if k > 0 else 1 - odd
            remote(zr.at[slot], zr.at[slot], z_send.at[0], z_recv.at[slot], up).wait_recv()
            total = total + zr[slot].astype(jnp.float32)
    total = total * gate_ref[...]
    n = o_ref.shape[1]
    for h in range(2):
        o_ref[h] = total[h * n : (h + 1) * n].astype(o_ref.dtype)
    for copy in copies:
        copy.wait_send()


def down_and_scatter(act, w_down, gate, collective_id):
    rows, depth = act.shape
    width = w_down.shape[1] // 16
    vmem = pl.BlockSpec(memory_space=pltpu.VMEM)
    kind = act.dtype
    return pl.pallas_call(
        down_body,
        out_shape=jax.ShapeDtypeStruct((2, width // 4, rows), kind),
        in_specs=[vmem] * 3,
        out_specs=vmem,
        scratch_shapes=[
            pltpu.VMEM((4, rows, width), kind),
            pltpu.VMEM((4, rows, width), kind),
            pltpu.VMEM((4, rows, width), kind),
            pltpu.VMEM((4, 2, rows // 2, width), kind),
            pltpu.VMEM((4, 2, 2, rows // 2, width), kind),
            pltpu.VMEM((4, 2, width // 2, rows), kind),
            pltpu.VMEM((2, width // 2, rows), jnp.float32),
            pltpu.VMEM((8, width // 2, rows), kind),
            pltpu.SemaphoreType.DMA((4, 2)),
            pltpu.SemaphoreType.DMA((4, 2)),
            pltpu.SemaphoreType.DMA((4, 2, 2)),
            pltpu.SemaphoreType.DMA((4, 2, 2)),
            pltpu.SemaphoreType.DMA((8,)),
            pltpu.SemaphoreType.DMA((8,)),
        ],
        compiler_params=pltpu.CompilerParams(
            collective_id=collective_id, has_side_effects=True, vmem_limit_bytes=48 * 2**20
        ),
        name="down_scatter",
    )(act, w_down, gate)


def block_factor(precision, cache_scale):
    factor = jnp.where(precision[:, None, :, None] == 1, cache_scale, 1.0)
    return jnp.repeat(factor, BLOCK_LEN, axis=2)


def attend(query, new_kv, cache, factor, lengths):
    rows = query.shape[0]
    heads_kv = new_kv.shape[2] // HEAD
    scale = HEAD ** (-0.5)
    queries = query.reshape(rows, heads_kv, GROUP, HEAD)
    keys = cache[:, 0].reshape(rows, CACHE, heads_kv, HEAD)
    values = cache[:, 1].reshape(rows, CACHE, heads_kv, HEAD)
    fresh = new_kv.reshape(rows, 2, heads_kv, HEAD)
    scores = jnp.einsum("rkgd,rpkd->rkgp", queries, keys, preferred_element_type=jnp.float32)
    scores = scores * jnp.transpose(factor[:, 0], (0, 2, 1))[:, :, None, :] * scale
    own = (
        jnp.einsum("rkgd,rkd->rkg", queries, fresh[:, 0], preferred_element_type=jnp.float32)
        * scale
    )
    live = jnp.arange(CACHE)[None, :] < lengths[:, None]
    scores = jnp.where(live[:, None, None, :], scores, -jnp.inf)
    top = jnp.maximum(jnp.max(scores, axis=3), own)
    weights = jnp.exp(scores - top[..., None])
    own_weight = jnp.exp(own - top)
    total = jnp.sum(weights, axis=3) + own_weight
    value_weight = (
        weights / total[..., None] * jnp.transpose(factor[:, 1], (0, 2, 1))[:, :, None, :]
    ).astype(jnp.bfloat16)
    own_prob = (own_weight / total).astype(jnp.bfloat16)
    result = jnp.einsum("rkgp,rpkd->rkgd", value_weight, values, preferred_element_type=jnp.float32)
    result = result + own_prob.astype(jnp.float32)[..., None] * fresh[:, 1][:, :, None, :].astype(
        jnp.float32
    )
    return result.reshape(rows, heads_kv * GROUP * HEAD).astype(jnp.bfloat16)


def contract_first(a, b, **kw):
    return lax.dot_general(
        a, b, (((0,), (0,)), ((), ())), preferred_element_type=jnp.float32, **kw
    )


def hand_off(cache, factor, mig_req, mig_blocks, replica_id):
    chosen_req = mig_req[replica_id]
    levels = lax.dynamic_index_in_dim(cache, chosen_req, 0, keepdims=False).astype(jnp.float32)
    scales = lax.dynamic_index_in_dim(factor, chosen_req, 0, keepdims=False)
    keep = jnp.arange(CACHE) < mig_blocks[replica_id] * BLOCK_LEN
    return jnp.where(keep[None, :, None], levels * scales, 0.0).astype(jnp.bfloat16)


def arrivals(everyones, mig_dest, replica_id):
    aimed = mig_dest == replica_id
    numbers = jnp.arange(mig_dest.shape[0])
    first = jnp.min(jnp.where(aimed, numbers, mig_dest.shape[0]))
    last = jnp.max(jnp.where(aimed, numbers, -1))
    rows = []
    for source, there in ((first, jnp.any(aimed)), (last, last > first)):
        row = lax.dynamic_index_in_dim(everyones, source, 0, keepdims=False)
        rows.append(jnp.where(there, row, jnp.zeros((), row.dtype)))
    return jnp.stack(rows)[None]


def local(
    stream_in,
    query,
    new_kv,
    cache,
    precision,
    cache_scale,
    lengths,
    w_heads,
    norm_gain,
    w_router,
    expert_choice,
    w_in,
    w_down,
    mig_dest,
    mig_req,
    mig_blocks,
):
    tokens, mine = stream_in.shape
    capacity = tokens // 2
    experts = w_router.shape[1]
    half = mine // 2
    ff = w_in.shape[3]
    replica_id = lax.axis_index("rep")
    expert = lax.axis_index("hx")

    factor = block_factor(precision, cache_scale)
    attended = attend(query, new_kv, cache, factor, lengths)
    split = attended.shape[1] // 2
    left, right = gather_all(
        [attended[:, :split], attended[:, split:]],
        [
            (0, None, ("z", "y"), ("two", "two"), 0),
            (1, None, ("y", "z"), ("two", "two"), 1),
        ],
        1,
        "gather_attended",
    )
    part = lax.dot_general(
        w_heads[:split],
        left.reshape(tokens, split),
        (((0,), (1,)), ((), ())),
        preferred_element_type=jnp.float32,
    ) + lax.dot_general(
        w_heads[split:],
        right.reshape(tokens, split),
        (((0,), (1,)), ((), ())),
        preferred_element_type=jnp.float32,
    )
    outgoing = hand_off(cache, factor, mig_req, mig_blocks, replica_id)
    parts, everyones = gather_all(
        [part.astype(jnp.bfloat16).reshape(2, half, tokens), outgoing],
        [
            (0, 0, ("x", "c"), ("ring", "ring"), 0),
            (0, 1, ("x", "c"), ("ring", "ring"), 1),
            (1, 0, ("z", "y"), ("ring", "ring"), 0),
            (1, 1, ("y", "z"), ("ring", "ring"), 1),
        ],
        2,
        "gather_heads",
    )
    arrived = arrivals(everyones, mig_dest, replica_id)
    hidden = stream_in.T.astype(jnp.float32) + jnp.sum(
        parts.reshape(experts, mine, tokens).astype(jnp.float32), axis=0
    )

    ids = jnp.arange(experts)
    choice = expert_choice.T
    names = (choice[None, 0, :] == ids[:, None]) | (choice[None, 1, :] == ids[:, None])
    order = jnp.arange(tokens)
    earlier = (order[:, None] < order[None, :]).astype(jnp.bfloat16)
    rank = jnp.dot(
        names.astype(jnp.bfloat16), earlier, preferred_element_type=jnp.float32
    ).astype(jnp.int32)
    slot_of = jnp.where(names, rank, -1)
    my_slot = lax.dynamic_index_in_dim(slot_of, expert, 0, keepdims=False)
    pick = my_slot[:, None] == jnp.arange(capacity)[None, :]

    gained = hidden * norm_gain[:, None]
    u_slots = jnp.dot(
        gained.astype(jnp.bfloat16), pick.astype(jnp.bfloat16), preferred_element_type=jnp.float32
    ).astype(jnp.bfloat16)
    squares = jnp.sum(hidden * hidden, axis=0)
    logits = contract_first(
        w_router.astype(jnp.float32), gained, precision=lax.Precision.HIGHEST
    )
    first = jnp.sum(jnp.where(choice[None, 0, :] == ids[:, None], logits, 0.0), axis=0)
    second = jnp.sum(jnp.where(choice[None, 1, :] == ids[:, None], logits, 0.0), axis=0)
    ahead = jnp.where(choice[0] == expert, first - second, second - first)
    extra = jnp.concatenate(
        [squares[None], ahead[None], jnp.zeros((6, tokens), jnp.float32)], axis=0
    )
    extra_slots = jnp.dot(extra, pick.astype(jnp.float32), precision=lax.Precision.HIGHEST)
    u_all, extra_all = gather_all(
        [u_slots.reshape(2, half, capacity), extra_slots],
        [
            (0, 0, ("z", "y"), ("ring", "ring"), 0),
            (0, 1, ("y", "z"), ("ring", "ring"), 1),
            (1, None, ("y", "z"), ("ring", "ring"), 0),
        ],
        3,
        "gather_rows",
    )
    sums = jnp.sum(extra_all, axis=0)
    inverse = lax.rsqrt(sums[0] / D + EPSILON)
    gate_of_slot = 1.0 / (1.0 + jnp.exp(-sums[1] * inverse))
    gate_up = contract_first(w_in[0].reshape(D, 2 * ff), u_all.reshape(D, capacity))
    gate_up = gate_up * inverse[None, :]
    act = (jax.nn.silu(gate_up[:ff]) * gate_up[ff:]).astype(jnp.bfloat16)
    weighted = down_and_scatter(act.T, w_down[0], gate_of_slot[None], 4)
    (everyone,) = gather_all(
        [weighted],
        [
            (0, 0, ("x", "c"), ("ring", "ring"), 0),
            (0, 1, ("x", "c"), ("ring", "ring"), 1),
        ],
        5,
        "gather_experts",
    )
    place = (slot_of[:, None, :] == jnp.arange(capacity)[None, :, None]).astype(jnp.bfloat16)
    moe = lax.dot_general(
        everyone.reshape(experts, mine, capacity),
        place,
        (((0, 2), (0, 1)), ((), ())),
        preferred_element_type=jnp.float32,
    )
    mixed = (hidden + moe).astype(jnp.bfloat16).T
    return (mixed, arrived)


def solution(mesh):
    placed = (
        P(None, "rep"),
        P("rep", "hx"),
        P("rep", None, "hx"),
        P("rep", None, None, "hx"),
        P("rep", None),
        P("rep", None, None, "hx"),
        P("rep"),
        P("hx", "rep"),
        P("rep"),
        P("rep", None),
        P(),
        P("hx", None, None, "rep"),
        P("hx", "rep", None),
        P(),
        P(),
        P(),
    )
    return jax.shard_map(
        local,
        mesh=mesh,
        in_specs=placed,
        out_specs=(P(None, "rep"), P("rep", None, None, None, "hx")),
        check_vma=False,
    )
```

```python
import functools

import jax
import jax.numpy as jnp
from jax import lax
from jax.experimental import pallas as pl
from jax.experimental.pallas import tpu as pltpu
from jax.sharding import PartitionSpec as P

D = 6144
HEAD = 128
GROUP = 6
BLOCK_LEN = 32
IN_MOST = 2
CACHE = 128
EPSILON = 1e-05

SIZES = {"y": 4, "z": 8, "x": 4, "c": 2}
PLANE = ("y", "z")
CHIPS = ("x", "c")


def coords():
    rep = lax.axis_index("rep")
    hx = lax.axis_index("hx")
    return {"y": rep // 8, "z": lax.rem(rep, 8), "x": hx // 2, "c": lax.rem(hx, 2)}


def device_at(at):
    return {"rep": at["y"] * 8 + at["z"], "hx": at["x"] * 2 + at["c"]}


def shifted(at, dim, step):
    n = SIZES[dim]
    moved = dict(at)
    moved[dim] = lax.rem(at[dim] + (step % n), n)
    return moved


def index_in(at, dims):
    if "y" in dims:
        return at["y"] * 8 + at["z"]
    return at["x"] * 2 + at["c"]


TREES = {
    "ring": {
        2: {0: (1,)},
        4: {0: (1, -1), 1: (2,)},
        8: {0: (1, -1), 1: (2,), 2: (3,), 3: (4,), -1: (-2,), -2: (-3,)},
    },
    "two": {
        2: {0: (1,)},
        4: {0: (1, -1, 2)},
        8: {0: (1, -1, 2, -2), 2: (3, 4), -2: (-3,)},
    },
    "direct": {
        2: {0: (1,)},
        4: {0: (1, -1, 2)},
        8: {0: (1, -1, 2, -2, 3, -3, 4)},
    },
}


def tree_of(kind, n, flip):
    sign = -1 if flip % 2 and n > 2 else 1
    return {sign * o: tuple(sign * t for t in to) for o, to in TREES[kind][n].items()}


def places_of(tree):
    found = [0]
    for o in found:
        found += tree.get(o, ())
    return found


def depth_of(tree, o):
    if o == 0:
        return 0
    return 1 + depth_of(tree, next(p for p, to in tree.items() if o in to))


def gather_plan(dims, kinds, flip):
    na, nb = SIZES[dims[0]], SIZES[dims[1]]
    ta = tree_of(kinds[0], na, flip)
    events = []
    for oa in places_of(ta):
        tb = tree_of(kinds[1], nb, oa + flip)
        for ob in places_of(tb):
            sends = []
            if ob == 0:
                sends += [(t, 0) for t in ta.get(oa, ())]
            sends += [(oa, t) for t in tb.get(ob, ())]
            cost = 3 * (depth_of(ta, oa) + depth_of(tb, ob)) + abs(oa) + abs(ob)
            events.append((cost, oa, ob, sends))
    return sorted(events, key=lambda e: e[0])


def partners(dims, kinds):
    found = {}
    for dim, kind in zip(dims, kinds):
        steps = found.setdefault(dim, set())
        for o, to in TREES[kind][SIZES[dim]].items():
            for t in to:
                steps |= {(t - o) % SIZES[dim], (o - t) % SIZES[dim]}
    return found


def greet(me, steps):
    barrier = pltpu.get_barrier_semaphore()
    count = 0
    for dim in sorted(steps):
        for step in sorted(steps[dim]):
            pl.semaphore_signal(
                barrier,
                inc=1,
                device_id=device_at(shifted(me, dim, step)),
                device_id_type=pl.DeviceIdType.MESH,
            )
            count += 1
    return lambda: pl.semaphore_wait(barrier, count)


def remote(source, place, send_sem, recv_sem, there):
    return pltpu.make_async_remote_copy(
        src_ref=source,
        dst_ref=place,
        send_sem=send_sem,
        recv_sem=recv_sem,
        device_id=device_at(there),
        device_id_type=pl.DeviceIdType.MESH,
    )


class Gather:
    def __init__(self, me, source, place, dims, kinds, flip, sems, base):
        self.me, self.source, self.place = me, source, place
        self.dims, self.kinds, self.flip = dims, kinds, flip
        self.send_sem, self.recv_sem, self.own_sem = sems
        self.plan = gather_plan(dims, kinds, flip)
        self.slots = {(oa, ob): base + k for k, (_, oa, ob, _) in enumerate(self.plan)}
        self.copies = []

    def at(self, oa, ob):
        origin = shifted(shifted(self.me, self.dims[0], -oa), self.dims[1], -ob)
        return self.place(index_in(origin, self.dims))

    def step(self, event):
        _, oa, ob, sends = event
        place = self.at(oa, ob)
        source = place
        if (oa, ob) == (0, 0):
            source = self.source
        else:
            slot = self.slots[oa, ob]
            near = shifted(self.me, self.dims[0], 1)
            remote(place, place, self.send_sem.at[0], self.recv_sem.at[slot], near).wait_recv()
        for to in sends:
            there = shifted(shifted(self.me, self.dims[0], to[0] - oa), self.dims[1], to[1] - ob)
            slot = self.slots[to]
            copy = remote(source, place, self.send_sem.at[slot], self.recv_sem.at[slot], there)
            copy.start()
            self.copies.append(copy)
        if (oa, ob) == (0, 0):
            self.own = pltpu.make_async_copy(source, place, self.own_sem)
            self.own.start()

    def finish(self):
        for copy in self.copies:
            copy.wait_send()


def run(*gathers):
    todo = [(e[0], n, e) for n, g in enumerate(gathers) for e in g.plan]
    for _, n, event in sorted(todo, key=lambda e: e[:2]):
        gathers[n].step(event)
    for g in gathers:
        g.own.wait()


def dot_f32(a, b):
    return jnp.dot(a, b, preferred_element_type=jnp.float32)


def split_three(x):
    high = x.astype(jnp.bfloat16)
    rest = x - high.astype(jnp.float32)
    middle = rest.astype(jnp.bfloat16)
    low = (rest - middle.astype(jnp.float32)).astype(jnp.bfloat16)
    return high, middle, low


def attend(scalars, q_ref, new_ref, cache_ref, left_ref, right_ref, queries, scores, weights):
    lengths, factor = scalars
    rows = q_ref.shape[0]
    scale = HEAD ** (-0.5)
    queries[...] = jnp.zeros_like(queries)
    for g in range(GROUP):
        queries[:, g, :] = q_ref[:, g * HEAD : (g + 1) * HEAD].astype(jnp.float32)
    lane = lax.broadcasted_iota(jnp.int32, (8, CACHE), 1)

    def along(j, r):
        row = jnp.full((8, CACHE), factor(j, 3, r))
        for b in (2, 1, 0):
            row = jnp.where(lane < (b + 1) * BLOCK_LEN, factor(j, b, r), row)
        return row

    for r in range(rows):
        raw = lax.dot_general(
            queries[r].astype(jnp.bfloat16),
            cache_ref[r, 0],
            (((1,), (1,)), ((), ())),
            preferred_element_type=jnp.float32,
        )
        scores[r] = jnp.where(lane < lengths[r], raw * along(0, r) * scale, -jnp.inf)
        weights[r] = along(1, r)
    fresh = new_ref[...].astype(jnp.float32)
    own = jnp.sum(queries[...] * fresh[:, 0:1, :], axis=2, keepdims=True) * scale
    s = scores[...]
    top = jnp.maximum(jnp.max(s, axis=2, keepdims=True), own)
    s = jnp.exp(s - top)
    own = jnp.exp(own - top)
    total = jnp.sum(s, axis=2, keepdims=True) + own
    weights[...] = s / total * weights[...]
    own = (own / total).astype(jnp.bfloat16).astype(jnp.float32) * fresh[:, 1:2, :]
    for r in range(rows):
        scores[r] = dot_f32(weights[r].astype(jnp.bfloat16), cache_ref[r, 1])
    scores[...] = scores[...] + own
    for g in range(GROUP):
        ref = left_ref if g < GROUP // 2 else right_ref
        at = g % (GROUP // 2)
        ref[:, at * HEAD : (at + 1) * HEAD] = scores[:, g, :].astype(ref.dtype)


def hand_off(cache_ref, factor, request, blocks, going_ref):
    for j in range(2):
        for b in range(CACHE // BLOCK_LEN):
            span = pl.ds(b * BLOCK_LEN, BLOCK_LEN)
            levels = cache_ref[request, j, span, :].astype(jnp.float32)
            going_ref[j, span, :] = jnp.where(
                b < blocks, levels * factor(j, b, request), 0.0
            ).astype(going_ref.dtype)


def route(choice_ref, slot_ref, pick_ref, expert):
    tokens = choice_ref.shape[1]
    experts = slot_ref.shape[0]
    ids = lax.broadcasted_iota(jnp.int32, (experts, tokens), 0)
    order = lax.broadcasted_iota(jnp.int32, (experts, tokens), 1)
    named = (choice_ref[0:1, :] == ids) | (choice_ref[1:2, :] == ids)
    count = named.astype(jnp.int32)
    step = 1
    while step < tokens:
        count = count + jnp.where(order >= step, pltpu.roll(count, step, 1), 0)
        step *= 2
    slots = jnp.where(named, count - 1, -1)
    slot_ref[...] = slots
    mine = jnp.sum(jnp.where(ids == expert, slots, 0).astype(jnp.float32).T, axis=1, keepdims=True)
    capacity = pick_ref.shape[1]
    across = lax.broadcasted_iota(jnp.int32, (tokens, capacity), 1).astype(jnp.float32)
    pick_ref[...] = (mine == across).astype(jnp.float32).astype(pick_ref.dtype)


def front_items():
    zy, yz, xc = ("z", "y"), ("y", "z"), ("x", "c")
    two, ring = ("two", "two"), ("ring", "ring")
    return {
        "left": (zy, two, 0),
        "right": (yz, two, 1),
        "part0": (xc, ring, 0),
        "part1": (xc, ring, 1),
        "going0": (zy, ring, 0),
        "going1": (yz, ring, 1),
        "rows0": (zy, ring, 0),
        "rows1": (yz, ring, 1),
        "extra": (yz, ring, 0),
    }


def members(item):
    return SIZES[item[0][0]] * SIZES[item[0][1]]


def front_body(*refs):
    hbm, outs, scratch = refs[:13], refs[13:18], refs[18:]
    u_ref, extra_ref, hidden_ref, came_ref, slot_ref = outs
    local_refs, scratch = scratch[:13], scratch[13:]
    (
        lengths,
        precision,
        scales,
        mig_req,
        mig_blocks,
        q_ref,
        new_ref,
        cache_ref,
        choice_ref,
        w_ref,
        stream_ref,
        gain_ref,
        router_ref,
    ) = local_refs
    (
        left_ref,
        right_ref,
        going_ref,
        pick_ref,
        queries,
        scores,
        weights,
        left_all,
        right_all,
        part_own,
        part_all,
        rows_own,
        extra_own,
        send_sem,
        recv_sem,
        own_sem,
        load_sem,
    ) = scratch
    me = coords()
    items = front_items()
    greeted = {}
    for dims, kinds, _ in items.values():
        for dim, steps in partners(dims, kinds).items():
            greeted.setdefault(dim, set()).update(steps)
    entered = greet(me, greeted)
    loads = [
        pltpu.make_async_copy(a, b, load_sem.at[k])
        for k, (a, b) in enumerate(zip(hbm, local_refs))
    ]
    for load in loads:
        load.start()

    def factor(j, b, r):
        return jnp.where(precision[b, r] == 1, scales[4 * j + b, r], 1.0)

    for load in loads[:8]:
        load.wait()
    attend(
        (lengths, factor), q_ref, new_ref, cache_ref, left_ref, right_ref, queries, scores, weights
    )
    rep = lax.axis_index("rep")
    entered()
    refs = {
        "left": (left_ref, lambda i: left_all.at[i]),
        "right": (right_ref, lambda i: right_all.at[i]),
        "part0": (part_own.at[0], lambda i: part_all.at[i, 0]),
        "part1": (part_own.at[1], lambda i: part_all.at[i, 1]),
        "going0": (going_ref.at[0], lambda i: came_ref.at[i, 0]),
        "going1": (going_ref.at[1], lambda i: came_ref.at[i, 1]),
        "rows0": (rows_own.at[0], lambda i: u_ref.at[i, 0]),
        "rows1": (rows_own.at[1], lambda i: u_ref.at[i, 1]),
        "extra": (extra_own, lambda i: extra_ref.at[i]),
    }
    g, base = {}, 0
    for n, (name, (dims, kinds, flip)) in enumerate(items.items()):
        sems = (send_sem, recv_sem, own_sem.at[n])
        g[name] = Gather(me, *refs[name], dims, kinds, flip, sems, base)
        base += members(items[name])
    moving = sorted(
        [(e[0], n, e) for n in (0, 1) for e in g["going%d" % n].plan], key=lambda e: e[:2]
    )

    def move(depth):
        while moving and moving[0][0] <= depth:
            _, n, event = moving.pop(0)
            g["going%d" % n].step(event)

    todo = sorted(
        [(e[0], n, e) for n, k in enumerate(("left", "right")) for e in g[k].plan],
        key=lambda e: e[:2],
    )
    for k, (cost, n, event) in enumerate(todo):
        if k == 2:
            hand_off(cache_ref, factor, mig_req[rep], mig_blocks[rep], going_ref)
            move(0)
            for load in loads[8:]:
                load.wait()
            route(choice_ref, slot_ref, pick_ref, lax.axis_index("hx"))
        g[("left", "right")[n]].step(event)
    for k in ("left", "right"):
        g[k].own.wait()

    split = left_ref.shape[1]
    tokens = stream_ref.shape[1]
    transposed = (((1,), (1,)), ((), ()))
    part = lax.dot_general(
        w_ref[:, :split],
        left_all[...].reshape(tokens, split),
        transposed,
        preferred_element_type=jnp.float32,
    ) + lax.dot_general(
        w_ref[:, split:],
        right_all[...].reshape(tokens, split),
        transposed,
        preferred_element_type=jnp.float32,
    )
    half = part_own.shape[1]
    for n in range(2):
        part_own[n] = part[n * half : (n + 1) * half].astype(part_own.dtype)
    todo = sorted(
        [(e[0], n, e) for n in range(2) for e in g["part%d" % n].plan], key=lambda e: e[:2]
    )
    for k, (cost, n, event) in enumerate(todo):
        if k == 2:
            move(4)
        if k == 6:
            move(8)
        g["part%d" % n].step(event)
    for k in ("part0", "part1"):
        g[k].own.wait()

    gain = jnp.broadcast_to(gain_ref[...], (8, gain_ref.shape[1])).T[:, :1]
    squares = jnp.zeros((1, tokens), jnp.float32)
    logits = jnp.zeros((router_ref.shape[0], tokens), jnp.float32)
    for n in range(2):
        span = pl.ds(n * half, half)
        hidden = stream_ref[span, :].astype(jnp.float32)
        for e in range(part_all.shape[0]):
            hidden = hidden + part_all[e, n].astype(jnp.float32)
        hidden_ref[span, :] = hidden
        gained = hidden * gain[n * half : (n + 1) * half]
        rows_own[n] = dot_f32(gained.astype(jnp.bfloat16), pick_ref[...]).astype(rows_own.dtype)
        g["rows%d" % n].step(g["rows%d" % n].plan.pop(0))
        squares = squares + jnp.sum(hidden * hidden, axis=0, keepdims=True)
        logits = logits + jnp.dot(
            router_ref[:, n * half : (n + 1) * half].astype(jnp.float32),
            gained,
            precision=lax.Precision.HIGHEST,
            preferred_element_type=jnp.float32,
        )
    ids = lax.broadcasted_iota(jnp.int32, logits.shape, 0)
    choice = choice_ref[...]
    first = jnp.sum(jnp.where(choice[0:1] == ids, logits, 0.0), axis=0, keepdims=True)
    second = jnp.sum(jnp.where(choice[1:2] == ids, logits, 0.0), axis=0, keepdims=True)
    ahead = jnp.where(choice[0:1] == lax.axis_index("hx"), first - second, second - first)
    terms = jnp.concatenate(
        [t.astype(jnp.float32) for t in split_three(squares) + split_three(ahead)]
        + [jnp.zeros((2, tokens), jnp.float32)],
        axis=0,
    ).astype(jnp.bfloat16)
    chosen = dot_f32(terms, pick_ref[...])
    extra_own[...] = jnp.concatenate(
        [
            chosen[0:1] + chosen[1:2] + chosen[2:3],
            chosen[3:4] + chosen[4:5] + chosen[5:6],
            chosen[2:8] * 0.0,
        ],
        axis=0,
    )
    move(11)
    todo = sorted(
        [(e[0], n, e) for n, k in enumerate(("rows0", "rows1", "extra")) for e in g[k].plan],
        key=lambda e: e[:2],
    )
    for cost, n, event in todo:
        if cost > 4:
            move(cost + 8)
        g[("rows0", "rows1", "extra")[n]].step(event)
    move(10**6)
    for k in ("rows0", "rows1", "extra", "going0", "going1"):
        g[k].own.wait()
    for k in g:
        g[k].finish()


def front(inputs, capacity, collective_id):
    query, stream = inputs[5], inputs[10]
    rows, wide = query.shape
    split = wide // 2
    mine, tokens = stream.shape
    half = mine // 2
    kind = query.dtype
    going = inputs[7].shape[1:]
    vmem = pl.BlockSpec(memory_space=pltpu.VMEM)
    anywhere = pl.BlockSpec(memory_space=pl.ANY)
    items = front_items()
    total = sum(members(item) for item in items.values())
    spaces = [pltpu.SMEM] * 5 + [pltpu.VMEM] * 8
    return pl.pallas_call(
        front_body,
        out_shape=[
            jax.ShapeDtypeStruct((32, 2, half, capacity), kind),
            jax.ShapeDtypeStruct((32, 8, capacity), jnp.float32),
            jax.ShapeDtypeStruct((mine, tokens), jnp.float32),
            jax.ShapeDtypeStruct((32, *going), kind),
            jax.ShapeDtypeStruct((8, tokens), jnp.int32),
        ],
        in_specs=[pl.BlockSpec(memory_space=pltpu.HBM)] * 13,
        out_specs=[anywhere, anywhere, vmem, anywhere, vmem],
        scratch_shapes=[space(x.shape, x.dtype) for space, x in zip(spaces, inputs)]
        + [
            pltpu.VMEM((rows, split), kind),
            pltpu.VMEM((rows, split), kind),
            pltpu.VMEM(going, kind),
            pltpu.VMEM((tokens, capacity), kind),
            pltpu.VMEM((rows, 8, HEAD), jnp.float32),
            pltpu.VMEM((rows, 8, HEAD), jnp.float32),
            pltpu.VMEM((rows, 8, HEAD), jnp.float32),
            pltpu.VMEM((32, rows, split), kind),
            pltpu.VMEM((32, rows, split), kind),
            pltpu.VMEM((2, half, tokens), kind),
            pltpu.VMEM((8, 2, half, tokens), kind),
            pltpu.VMEM((2, half, capacity), kind),
            pltpu.VMEM((8, capacity), jnp.float32),
            pltpu.SemaphoreType.DMA((total,)),
            pltpu.SemaphoreType.DMA((total,)),
            pltpu.SemaphoreType.DMA((len(items),)),
            pltpu.SemaphoreType.DMA((13,)),
        ],
        compiler_params=pltpu.CompilerParams(
            collective_id=collective_id, has_side_effects=True, vmem_limit_bytes=40 * 2**20
        ),
        name="front",
    )(*inputs)


def down_body(
    act_ref,
    w_hbm,
    gate_ref,
    hidden_hbm,
    slot_ref,
    came_hbm,
    dest_hbm,
    o_ref,
    arrived_ref,
    w_ref,
    hidden_ref,
    came_ref,
    dest_ref,
    p2,
    p1,
    pm,
    r1,
    fin,
    turned,
    tf,
    zr,
    place,
    out_own,
    out_all,
    *sems,
):
    s1_send, s1_recv, s2_send, s2_recv, z_send, z_recv, x_send, x_recv, x_own, load_sem = sems
    me = coords()
    xc, kinds = ("x", "c"), ("ring", "ring")
    entered = greet(me, {"y": {1, 3}, "z": set(range(1, 8)), **partners(xc, kinds)})
    group = w_ref.shape[1] // 4
    loads = {}
    for k, step in enumerate((2, 1, 3, 0)):
        start = pl.multiple_of(lax.rem(me["y"] + step, 4) * group, 128)
        span = pl.ds(start, group)
        loads[step] = pltpu.make_async_copy(w_hbm.at[:, span], w_ref.at[:, span], load_sem.at[k])
        loads[step].start()
    late = [
        pltpu.make_async_copy(a, b, load_sem.at[4 + k])
        for k, (a, b) in enumerate(
            ((hidden_hbm, hidden_ref), (came_hbm, came_ref), (dest_hbm, dest_ref))
        )
    ]
    up, down = shifted(me, "y", 1), shifted(me, "y", -1)
    pair, odd = me["z"] // 2, lax.rem(me["z"], 2)
    rows = act_ref.shape[0]
    mid = rows // 2
    wide = w_ref.shape[1] // 16
    low, high = pl.ds(0, mid), pl.ds(mid, mid)
    order = (2, 1, 3, 0)

    def product(step, k):
        there = lax.rem(me["y"] + step, 4)
        start = there * (4 * wide) + lax.rem(pair + k, 4) * wide
        return dot_f32(act_ref[...], w_ref[:, pl.ds(pl.multiple_of(start, 128), wide)])

    copies = []

    def send(source, place, ss, rs, there):
        copy = remote(source, place, ss, rs, there)
        copy.start()
        copies.append(copy)
        return copy

    steps = {}
    loads[2].wait()
    for k in order:
        p2[k] = product(2, k).astype(p2.dtype)
        if k == order[0]:
            entered()
        a = send(p2.at[k, low], r1.at[k, 0], s1_send.at[k, 0], s1_recv.at[k, 0], up)
        b = send(p2.at[k, high], r1.at[k, 1], s1_send.at[k, 1], s1_recv.at[k, 1], down)
        steps[k] = (a, b)
    tokens = slot_ref.shape[1]
    down_rows = lax.broadcasted_iota(jnp.int32, (rows, tokens), 0)

    def place_expert(e):
        place[e] = (slot_ref[e : e + 1, :] == down_rows).astype(jnp.float32).astype(place.dtype)

    lasts = {}
    loads[1].wait()
    loads[3].wait()
    for load in late:
        load.start()
    for k in order:
        p1[k] = product(1, k).astype(p1.dtype)
        c = send(p1.at[k, high], fin.at[k, 0, 1], s2_send.at[k, 0, 1], s2_recv.at[k, 0, 1], up)
        pm[k] = product(3, k).astype(pm.dtype)
        d = send(pm.at[k, low], fin.at[k, 1, 0], s2_send.at[k, 1, 0], s2_recv.at[k, 1, 0], down)
        steps[k][0].wait_recv()
        p1[k, low] = (p1[k, low].astype(jnp.float32) + r1[k, 0].astype(jnp.float32)).astype(p1.dtype)
        e = send(p1.at[k, low], fin.at[k, 0, 0], s2_send.at[k, 0, 0], s2_recv.at[k, 0, 0], up)
        steps[k][1].wait_recv()
        pm[k, high] = (pm[k, high].astype(jnp.float32) + r1[k, 1].astype(jnp.float32)).astype(
            pm.dtype
        )
        f = send(pm.at[k, high], fin.at[k, 1, 1], s2_send.at[k, 1, 1], s2_recv.at[k, 1, 1], down)
        lasts[k] = (c, d, e, f)
    loads[0].wait()
    for load in late:
        load.wait()
    rep = lax.axis_index("rep")
    n_rep = dest_ref.shape[0]
    first, last = jnp.int32(n_rep), jnp.int32(-1)
    for source in range(n_rep):
        aimed = dest_ref[source] == rep
        first = jnp.where(aimed, jnp.minimum(first, source), first)
        last = jnp.where(aimed, source, last)
    for q, (source, there) in enumerate(((first, last >= 0), (last, last > first))):
        block = came_ref[jnp.clip(source, 0, n_rep - 1)].astype(jnp.float32)
        arrived_ref[0, q] = jnp.where(there, block, 0.0).astype(arrived_ref.dtype)
    for k in order:
        whole = product(0, k)
        for copy in lasts[k]:
            copy.wait_recv()
        whole = whole + jnp.concatenate(
            [
                fin[k, 0, 0].astype(jnp.float32) + fin[k, 1, 0].astype(jnp.float32),
                fin[k, 0, 1].astype(jnp.float32) + fin[k, 1, 1].astype(jnp.float32),
            ],
            axis=0,
        )
        whole = whole.T
        for e in range(2):
            part = whole[e * (wide // 2) : (e + 1) * (wide // 2)]
            turned[k, e] = part.astype(turned.dtype)
            if k == 0:
                tf[e] = part
        first = 2 * lax.rem(pair + k, 4)
        for e in range(2):
            if k > 0:
                there = dict(me, z=first + e)
                send(
                    turned.at[k, e],
                    zr.at[2 * k + odd],
                    z_send.at[2 * k + e],
                    z_recv.at[2 * k + odd],
                    there,
                )
        if k == 0:
            there = dict(me, z=first + 1 - odd)
            send(turned.at[0, 1 - odd], zr.at[odd], z_send.at[0], z_recv.at[odd], there)
    total = tf[odd]
    for k in order:
        for e in range(2) if k > 0 else (0,):
            slot = 2 * k + e if k > 0 else 1 - odd
            remote(zr.at[slot], zr.at[slot], z_send.at[0], z_recv.at[slot], up).wait_recv()
            total = total + zr[slot].astype(jnp.float32)
    total = total * gate_ref[...]
    n = out_own.shape[1]
    across = []
    for h in range(2):
        out_own[h] = total[h * n : (h + 1) * n].astype(out_own.dtype)
        across.append(
            Gather(
                me,
                out_own.at[h],
                lambda i, h=h: out_all.at[i, h],
                xc,
                kinds,
                h,
                (x_send, x_recv, x_own.at[h]),
                8 * h,
            )
        )
    for gather in across:
        gather.step(gather.plan.pop(0))
    for e in range(8):
        place_expert(e)
    run(*across)
    for h in range(2):
        span = pl.ds(h * n, n)
        mixed = hidden_ref[span, :]
        for e in range(8):
            mixed = mixed + dot_f32(out_all[e, h], place[e])
        o_ref[span, :] = mixed.astype(o_ref.dtype)
    for copy in copies:
        copy.wait_send()
    for gather in across:
        gather.finish()


def down_and_scatter(act, w_down, gate, hidden, slots, came, mig_dest, collective_id):
    rows, depth = act.shape
    width = w_down.shape[1] // 16
    vmem = pl.BlockSpec(memory_space=pltpu.VMEM)
    hbm = pl.BlockSpec(memory_space=pltpu.HBM)
    kind = act.dtype
    return pl.pallas_call(
        down_body,
        out_shape=[
            jax.ShapeDtypeStruct(hidden.shape, kind),
            jax.ShapeDtypeStruct((1, IN_MOST, *came.shape[1:]), kind),
        ],
        in_specs=[vmem, hbm, vmem, hbm, vmem, hbm, hbm],
        out_specs=[vmem, vmem],
        scratch_shapes=[
            pltpu.VMEM(w_down.shape, kind),
            pltpu.VMEM(hidden.shape, hidden.dtype),
            pltpu.VMEM(came.shape, kind),
            pltpu.SMEM(mig_dest.shape, mig_dest.dtype),
            pltpu.VMEM((4, rows, width), kind),
            pltpu.VMEM((4, rows, width), kind),
            pltpu.VMEM((4, rows, width), kind),
            pltpu.VMEM((4, 2, rows // 2, width), kind),
            pltpu.VMEM((4, 2, 2, rows // 2, width), kind),
            pltpu.VMEM((4, 2, width // 2, rows), kind),
            pltpu.VMEM((2, width // 2, rows), jnp.float32),
            pltpu.VMEM((8, width // 2, rows), kind),
            pltpu.VMEM((8, rows, slots.shape[1]), kind),
            pltpu.VMEM((2, width // 4, rows), kind),
            pltpu.VMEM((8, 2, width // 4, rows), kind),
            pltpu.SemaphoreType.DMA((4, 2)),
            pltpu.SemaphoreType.DMA((4, 2)),
            pltpu.SemaphoreType.DMA((4, 2, 2)),
            pltpu.SemaphoreType.DMA((4, 2, 2)),
            pltpu.SemaphoreType.DMA((8,)),
            pltpu.SemaphoreType.DMA((8,)),
            pltpu.SemaphoreType.DMA((16,)),
            pltpu.SemaphoreType.DMA((16,)),
            pltpu.SemaphoreType.DMA((2,)),
            pltpu.SemaphoreType.DMA((7,)),
        ],
        compiler_params=pltpu.CompilerParams(
            collective_id=collective_id, has_side_effects=True, vmem_limit_bytes=56 * 2**20
        ),
        name="down_scatter",
    )(act, w_down, gate, hidden, slots, came, mig_dest)


def contract_first(a, b, **kw):
    return lax.dot_general(
        a, b, (((0,), (0,)), ((), ())), preferred_element_type=jnp.float32, **kw
    )


def local(
    stream_in,
    query,
    new_kv,
    cache,
    precision,
    cache_scale,
    lengths,
    w_heads,
    norm_gain,
    w_router,
    expert_choice,
    w_in,
    w_down,
    mig_dest,
    mig_req,
    mig_blocks,
):
    tokens = stream_in.shape[0]
    capacity = tokens // 2
    ff = w_in.shape[3]
    choice = expert_choice.T
    rows = query.shape[0]
    u_all, extra_all, hidden, came, slots = front(
        [
            lengths,
            precision.T,
            jnp.transpose(cache_scale[..., 0], (1, 2, 0)).reshape(-1, rows),
            mig_req,
            mig_blocks,
            query,
            new_kv,
            cache,
            choice,
            w_heads.T,
            stream_in.T,
            norm_gain[None],
            w_router.T,
        ],
        capacity,
        1,
    )
    sums = jnp.sum(extra_all, axis=0)
    inverse = lax.rsqrt(sums[0] / D + EPSILON)
    gate_of_slot = 1.0 / (1.0 + jnp.exp(-sums[1] * inverse))
    gate_up = contract_first(w_in[0].reshape(D, 2 * ff), u_all.reshape(D, capacity))
    gate_up = gate_up * inverse[None, :]
    act = (jax.nn.silu(gate_up[:ff]) * gate_up[ff:]).astype(jnp.bfloat16)
    mixed, arrived = down_and_scatter(
        act.T, w_down[0], gate_of_slot[None], hidden, slots, came, mig_dest, 2
    )
    return (mixed.T, arrived)


def solution(mesh):
    placed = (
        P(None, "rep"),
        P("rep", "hx"),
        P("rep", None, "hx"),
        P("rep", None, None, "hx"),
        P("rep", None),
        P("rep", None, None, "hx"),
        P("rep"),
        P("hx", "rep"),
        P("rep"),
        P("rep", None),
        P(),
        P("hx", None, None, "rep"),
        P("hx", "rep", None),
        P(),
        P(),
        P(),
    )
    return jax.shard_map(
        local,
        mesh=mesh,
        in_specs=placed,
        out_specs=(P(None, "rep"), P("rep", None, None, None, "hx")),
        check_vma=False,
    )
```

```python
import functools

import jax
import jax.numpy as jnp
from jax import lax
from jax.experimental import pallas as pl
from jax.experimental.pallas import tpu as pltpu
from jax.sharding import PartitionSpec as P

D = 6144
HEAD = 128
GROUP = 6
BLOCK_LEN = 32
IN_MOST = 2
CACHE = 128
EPSILON = 1e-05

SIZES = {"y": 4, "z": 8, "x": 4, "c": 2}
PLANE = ("y", "z")
CHIPS = ("x", "c")


def coords():
    rep = lax.axis_index("rep")
    hx = lax.axis_index("hx")
    return {"y": rep // 8, "z": lax.rem(rep, 8), "x": hx // 2, "c": lax.rem(hx, 2)}


def device_at(at):
    return {"rep": at["y"] * 8 + at["z"], "hx": at["x"] * 2 + at["c"]}


def shifted(at, dim, step):
    n = SIZES[dim]
    moved = dict(at)
    moved[dim] = lax.rem(at[dim] + (step % n), n)
    return moved


def index_in(at, dims):
    if "y" in dims:
        return at["y"] * 8 + at["z"]
    return at["x"] * 2 + at["c"]


TREES = {
    "ring": {
        2: {0: (1,)},
        4: {0: (1, -1), 1: (2,)},
        8: {0: (1, -1), 1: (2,), 2: (3,), 3: (4,), -1: (-2,), -2: (-3,)},
    },
    "two": {
        2: {0: (1,)},
        4: {0: (1, -1, 2)},
        8: {0: (1, -1, 2, -2), 2: (3, 4), -2: (-3,)},
    },
    "direct": {
        2: {0: (1,)},
        4: {0: (1, -1, 2)},
        8: {0: (1, -1, 2, -2, 3, -3, 4)},
    },
}


def tree_of(kind, n, flip):
    sign = -1 if flip % 2 and n > 2 else 1
    return {sign * o: tuple(sign * t for t in to) for o, to in TREES[kind][n].items()}


def places_of(tree):
    found = [0]
    for o in found:
        found += tree.get(o, ())
    return found


def depth_of(tree, o):
    if o == 0:
        return 0
    return 1 + depth_of(tree, next(p for p, to in tree.items() if o in to))


def gather_plan(dims, kinds, flip):
    na, nb = SIZES[dims[0]], SIZES[dims[1]]
    ta = tree_of(kinds[0], na, flip)
    events = []
    for oa in places_of(ta):
        tb = tree_of(kinds[1], nb, oa + flip)
        for ob in places_of(tb):
            sends = []
            if ob == 0:
                sends += [(t, 0) for t in ta.get(oa, ())]
            sends += [(oa, t) for t in tb.get(ob, ())]
            cost = 3 * (depth_of(ta, oa) + depth_of(tb, ob)) + abs(oa) + abs(ob)
            events.append((cost, oa, ob, sends))
    return sorted(events, key=lambda e: e[0])


def partners(dims, kinds):
    found = {}
    for dim, kind in zip(dims, kinds):
        steps = found.setdefault(dim, set())
        for o, to in TREES[kind][SIZES[dim]].items():
            for t in to:
                steps |= {(t - o) % SIZES[dim], (o - t) % SIZES[dim]}
    return found


def greet(me, steps):
    barrier = pltpu.get_barrier_semaphore()
    count = 0
    for dim in sorted(steps):
        for step in sorted(steps[dim]):
            pl.semaphore_signal(
                barrier,
                inc=1,
                device_id=device_at(shifted(me, dim, step)),
                device_id_type=pl.DeviceIdType.MESH,
            )
            count += 1
    return lambda: pl.semaphore_wait(barrier, count)


def remote(source, place, send_sem, recv_sem, there):
    return pltpu.make_async_remote_copy(
        src_ref=source,
        dst_ref=place,
        send_sem=send_sem,
        recv_sem=recv_sem,
        device_id=device_at(there),
        device_id_type=pl.DeviceIdType.MESH,
    )


class Gather:
    def __init__(self, me, source, place, dims, kinds, flip, sems, base):
        self.me, self.source, self.place = me, source, place
        self.dims, self.kinds, self.flip = dims, kinds, flip
        self.send_sem, self.recv_sem, self.own_sem = sems
        self.plan = gather_plan(dims, kinds, flip)
        self.slots = {(oa, ob): base + k for k, (_, oa, ob, _) in enumerate(self.plan)}
        self.copies = []

    def at(self, oa, ob):
        origin = shifted(shifted(self.me, self.dims[0], -oa), self.dims[1], -ob)
        return self.place(index_in(origin, self.dims))

    def step(self, event):
        _, oa, ob, sends = event
        place = self.at(oa, ob)
        source = place
        if (oa, ob) == (0, 0):
            source = self.source
        else:
            slot = self.slots[oa, ob]
            near = shifted(self.me, self.dims[0], 1)
            remote(place, place, self.send_sem.at[0], self.recv_sem.at[slot], near).wait_recv()
        for to in sends:
            there = shifted(shifted(self.me, self.dims[0], to[0] - oa), self.dims[1], to[1] - ob)
            slot = self.slots[to]
            copy = remote(source, place, self.send_sem.at[slot], self.recv_sem.at[slot], there)
            copy.start()
            self.copies.append(copy)
        if (oa, ob) == (0, 0):
            self.own = pltpu.make_async_copy(source, place, self.own_sem)
            self.own.start()

    def finish(self):
        for copy in self.copies:
            copy.wait_send()


def run(*gathers):
    todo = [(e[0], n, e) for n, g in enumerate(gathers) for e in g.plan]
    for _, n, event in sorted(todo, key=lambda e: e[:2]):
        gathers[n].step(event)
    for g in gathers:
        g.own.wait()


def dot_f32(a, b):
    return jnp.dot(a, b, preferred_element_type=jnp.float32)


def split_three(x):
    high = x.astype(jnp.bfloat16)
    rest = x - high.astype(jnp.float32)
    middle = rest.astype(jnp.bfloat16)
    low = (rest - middle.astype(jnp.float32)).astype(jnp.bfloat16)
    return high, middle, low


def attend(scalars, q_ref, new_ref, cache_ref, left_ref, right_ref, queries, scores, weights):
    lengths, factor = scalars
    rows = q_ref.shape[0]
    scale = HEAD ** (-0.5)
    queries[...] = jnp.zeros_like(queries)
    for g in range(GROUP):
        queries[:, g, :] = q_ref[:, g * HEAD : (g + 1) * HEAD].astype(jnp.float32)
    lane = lax.broadcasted_iota(jnp.int32, (8, CACHE), 1)

    def along(j, r):
        row = jnp.full((8, CACHE), factor(j, 3, r))
        for b in (2, 1, 0):
            row = jnp.where(lane < (b + 1) * BLOCK_LEN, factor(j, b, r), row)
        return row

    for r in range(rows):
        raw = lax.dot_general(
            queries[r].astype(jnp.bfloat16),
            cache_ref[r, 0],
            (((1,), (1,)), ((), ())),
            preferred_element_type=jnp.float32,
        )
        scores[r] = jnp.where(lane < lengths[r], raw * along(0, r) * scale, -jnp.inf)
        weights[r] = along(1, r)
    fresh = new_ref[...].astype(jnp.float32)
    own = jnp.sum(queries[...] * fresh[:, 0:1, :], axis=2, keepdims=True) * scale
    s = scores[...]
    top = jnp.maximum(jnp.max(s, axis=2, keepdims=True), own)
    s = jnp.exp(s - top)
    own = jnp.exp(own - top)
    total = jnp.sum(s, axis=2, keepdims=True) + own
    weights[...] = s / total * weights[...]
    own = (own / total).astype(jnp.bfloat16).astype(jnp.float32) * fresh[:, 1:2, :]
    for r in range(rows):
        scores[r] = dot_f32(weights[r].astype(jnp.bfloat16), cache_ref[r, 1])
    scores[...] = scores[...] + own
    for g in range(GROUP):
        ref = left_ref if g < GROUP // 2 else right_ref
        at = g % (GROUP // 2)
        ref[:, at * HEAD : (at + 1) * HEAD] = scores[:, g, :].astype(ref.dtype)


def hand_off(cache_ref, factor, request, blocks, going_ref):
    for j in range(2):
        for b in range(CACHE // BLOCK_LEN):
            span = pl.ds(b * BLOCK_LEN, BLOCK_LEN)
            levels = cache_ref[request, j, span, :].astype(jnp.float32)
            going_ref[j, span, :] = jnp.where(
                b < blocks, levels * factor(j, b, request), 0.0
            ).astype(going_ref.dtype)


def route(choice_ref, slot_ref, pick_ref, expert):
    tokens = choice_ref.shape[1]
    experts = slot_ref.shape[0]
    ids = lax.broadcasted_iota(jnp.int32, (experts, tokens), 0)
    order = lax.broadcasted_iota(jnp.int32, (experts, tokens), 1)
    named = (choice_ref[0:1, :] == ids) | (choice_ref[1:2, :] == ids)
    count = named.astype(jnp.int32)
    step = 1
    while step < tokens:
        count = count + jnp.where(order >= step, pltpu.roll(count, step, 1), 0)
        step *= 2
    slots = jnp.where(named, count - 1, -1)
    slot_ref[...] = slots
    mine = jnp.sum(jnp.where(ids == expert, slots, 0).astype(jnp.float32).T, axis=1, keepdims=True)
    capacity = pick_ref.shape[1]
    across = lax.broadcasted_iota(jnp.int32, (tokens, capacity), 1).astype(jnp.float32)
    pick_ref[...] = (mine == across).astype(jnp.float32).astype(pick_ref.dtype)


def front_items():
    zy, yz, xc = ("z", "y"), ("y", "z"), ("x", "c")
    two, ring = ("two", "two"), ("ring", "ring")
    return {
        "left": (zy, two, 0),
        "right": (yz, two, 1),
        **{"part%d" % n: (xc, ring, n) for n in range(4)},
        "going0": (zy, ring, 0),
        "going1": (yz, ring, 1),
        **{"rows%d" % n: (zy if n % 2 == 0 else yz, ring, n // 2 + n % 2) for n in range(4)},
        "extra": (yz, ring, 0),
    }


PIECES = ((0, 64), (64, 32), (96, 48), (144, 48))
PARTS = ((0, 48), (48, 48), (96, 48), (144, 48))


def members(item):
    return SIZES[item[0][0]] * SIZES[item[0][1]]


def front_body(*refs):
    hbm, outs, scratch = refs[:13], refs[13:18], refs[18:]
    u_ref, extra_ref, hidden_ref, came_ref, slot_ref = outs
    local_refs, scratch = scratch[:13], scratch[13:]
    (
        lengths,
        precision,
        scales,
        mig_req,
        mig_blocks,
        q_ref,
        new_ref,
        cache_ref,
        choice_ref,
        w_ref,
        stream_ref,
        gain_ref,
        router_ref,
    ) = local_refs
    (
        left_ref,
        right_ref,
        going_ref,
        pick_ref,
        queries,
        scores,
        weights,
        left_all,
        right_all,
        part_own,
        part_all,
        rows_own,
        extra_own,
        send_sem,
        recv_sem,
        own_sem,
        load_sem,
    ) = scratch
    me = coords()
    items = front_items()
    greeted = {}
    for dims, kinds, _ in items.values():
        for dim, steps in partners(dims, kinds).items():
            greeted.setdefault(dim, set()).update(steps)
    entered = greet(me, greeted)
    loads = [
        pltpu.make_async_copy(a, b, load_sem.at[k])
        for k, (a, b) in enumerate(zip(hbm, local_refs))
    ]
    for load in loads:
        load.start()

    def factor(j, b, r):
        return jnp.where(precision[b, r] == 1, scales[4 * j + b, r], 1.0)

    for load in loads[:8]:
        load.wait()
    attend(
        (lengths, factor), q_ref, new_ref, cache_ref, left_ref, right_ref, queries, scores, weights
    )
    rep = lax.axis_index("rep")
    entered()
    refs = {
        "left": (left_ref, lambda i: left_all.at[i]),
        "right": (right_ref, lambda i: right_all.at[i]),
        **{
            "part%d" % n: (
                part_own.at[pl.ds(*piece)],
                lambda i, piece=piece: part_all.at[i, pl.ds(*piece)],
            )
            for n, piece in enumerate(PARTS)
        },
        "going0": (going_ref.at[0], lambda i: came_ref.at[i, 0]),
        "going1": (going_ref.at[1], lambda i: came_ref.at[i, 1]),
        **{
            "rows%d" % n: (
                rows_own.at[pl.ds(*piece)],
                lambda i, piece=piece: u_ref.at[i, pl.ds(*piece)],
            )
            for n, piece in enumerate(PIECES)
        },
        "extra": (extra_own, lambda i: extra_ref.at[i]),
    }
    g, base = {}, 0
    for n, (name, (dims, kinds, flip)) in enumerate(items.items()):
        sems = (send_sem, recv_sem, own_sem.at[n])
        g[name] = Gather(me, *refs[name], dims, kinds, flip, sems, base)
        base += members(items[name])
    moving = sorted(
        [(e[0], n, e) for n in (0, 1) for e in g["going%d" % n].plan], key=lambda e: e[:2]
    )

    def move(depth):
        while moving and moving[0][0] <= depth:
            _, n, event = moving.pop(0)
            g["going%d" % n].step(event)

    todo = sorted(
        [(e[0], n, e) for n, k in enumerate(("left", "right")) for e in g[k].plan],
        key=lambda e: e[:2],
    )
    for k, (cost, n, event) in enumerate(todo):
        if k == 2:
            hand_off(cache_ref, factor, mig_req[rep], mig_blocks[rep], going_ref)
            move(0)
            for load in loads[8:]:
                load.wait()
            route(choice_ref, slot_ref, pick_ref, lax.axis_index("hx"))
        g[("left", "right")[n]].step(event)
    for k in ("left", "right"):
        g[k].own.wait()

    split = left_ref.shape[1]
    tokens = stream_ref.shape[1]
    transposed = (((1,), (1,)), ((), ()))
    half = stream_ref.shape[0] // 2
    for n in range(2):
        span = pl.ds(n * half, half)
        part = lax.dot_general(
            w_ref[span, :split],
            left_all[...].reshape(tokens, split),
            transposed,
            preferred_element_type=jnp.float32,
        ) + lax.dot_general(
            w_ref[span, split:],
            right_all[...].reshape(tokens, split),
            transposed,
            preferred_element_type=jnp.float32,
        )
        part_own[span, :] = part.astype(part_own.dtype)
        for k in (2 * n, 2 * n + 1):
            g["part%d" % k].step(g["part%d" % k].plan.pop(0))
    move(4)

    def early(n):
        names = ["part%d" % k for k in (2 * n, 2 * n + 1)]
        found = sorted([(e[0], k, e) for k in names for e in g[k].plan], key=lambda e: e[:2])
        for _, k, event in found:
            g[k].step(event)
        for k in names:
            g[k].own.wait()
        move(8)

    gain = jnp.broadcast_to(gain_ref[...], (8, gain_ref.shape[1])).T[:, :1]
    squares = jnp.zeros((1, tokens), jnp.float32)
    logits = jnp.zeros((router_ref.shape[0], tokens), jnp.float32)
    for n in range(2):
        span = pl.ds(n * half, half)
        early(n)
        hidden = stream_ref[span, :].astype(jnp.float32)
        for e in range(part_all.shape[0]):
            hidden = hidden + part_all[e, span, :].astype(jnp.float32)
        hidden_ref[span, :] = hidden
        gained = hidden * gain[n * half : (n + 1) * half]
        rows_own[span, :] = dot_f32(gained.astype(jnp.bfloat16), pick_ref[...]).astype(
            rows_own.dtype
        )
        for k in (2 * n, 2 * n + 1):
            g["rows%d" % k].step(g["rows%d" % k].plan.pop(0))
        squares = squares + jnp.sum(hidden * hidden, axis=0, keepdims=True)
        logits = logits + jnp.dot(
            router_ref[:, n * half : (n + 1) * half].astype(jnp.float32),
            gained,
            precision=lax.Precision.HIGHEST,
            preferred_element_type=jnp.float32,
        )
    ids = lax.broadcasted_iota(jnp.int32, logits.shape, 0)
    choice = choice_ref[...]
    first = jnp.sum(jnp.where(choice[0:1] == ids, logits, 0.0), axis=0, keepdims=True)
    second = jnp.sum(jnp.where(choice[1:2] == ids, logits, 0.0), axis=0, keepdims=True)
    ahead = jnp.where(choice[0:1] == lax.axis_index("hx"), first - second, second - first)
    terms = jnp.concatenate(
        [t.astype(jnp.float32) for t in split_three(squares) + split_three(ahead)]
        + [jnp.zeros((2, tokens), jnp.float32)],
        axis=0,
    ).astype(jnp.bfloat16)
    chosen = dot_f32(terms, pick_ref[...])
    extra_own[...] = jnp.concatenate(
        [
            chosen[0:1] + chosen[1:2] + chosen[2:3],
            chosen[3:4] + chosen[4:5] + chosen[5:6],
            chosen[2:8] * 0.0,
        ],
        axis=0,
    )
    move(11)
    last = ("rows0", "rows1", "rows2", "rows3", "extra")
    todo = sorted(
        [(e[0], n, e) for n, k in enumerate(last) for e in g[k].plan],
        key=lambda e: e[:2],
    )
    for cost, n, event in todo:
        if cost > 8:
            move(cost + 2)
        g[last[n]].step(event)
    move(10**6)
    for k in (*last, "going0", "going1"):
        g[k].own.wait()
    for k in g:
        g[k].finish()


def front(inputs, capacity, collective_id):
    query, stream = inputs[5], inputs[10]
    rows, wide = query.shape
    split = wide // 2
    mine, tokens = stream.shape
    half = mine // 2
    kind = query.dtype
    going = inputs[7].shape[1:]
    vmem = pl.BlockSpec(memory_space=pltpu.VMEM)
    anywhere = pl.BlockSpec(memory_space=pl.ANY)
    items = front_items()
    total = sum(members(item) for item in items.values())
    spaces = [pltpu.SMEM] * 5 + [pltpu.VMEM] * 8
    return pl.pallas_call(
        front_body,
        out_shape=[
            jax.ShapeDtypeStruct((32, mine, capacity), kind),
            jax.ShapeDtypeStruct((32, 8, capacity), jnp.float32),
            jax.ShapeDtypeStruct((mine, tokens), jnp.float32),
            jax.ShapeDtypeStruct((32, *going), kind),
            jax.ShapeDtypeStruct((8, tokens), jnp.int32),
        ],
        in_specs=[pl.BlockSpec(memory_space=pltpu.HBM)] * 13,
        out_specs=[anywhere, anywhere, vmem, anywhere, vmem],
        scratch_shapes=[space(x.shape, x.dtype) for space, x in zip(spaces, inputs)]
        + [
            pltpu.VMEM((rows, split), kind),
            pltpu.VMEM((rows, split), kind),
            pltpu.VMEM(going, kind),
            pltpu.VMEM((tokens, capacity), kind),
            pltpu.VMEM((rows, 8, HEAD), jnp.float32),
            pltpu.VMEM((rows, 8, HEAD), jnp.float32),
            pltpu.VMEM((rows, 8, HEAD), jnp.float32),
            pltpu.VMEM((32, rows, split), kind),
            pltpu.VMEM((32, rows, split), kind),
            pltpu.VMEM((mine, tokens), kind),
            pltpu.VMEM((8, mine, tokens), kind),
            pltpu.VMEM((mine, capacity), kind),
            pltpu.VMEM((8, capacity), jnp.float32),
            pltpu.SemaphoreType.DMA((total,)),
            pltpu.SemaphoreType.DMA((total,)),
            pltpu.SemaphoreType.DMA((len(items),)),
            pltpu.SemaphoreType.DMA((13,)),
        ],
        compiler_params=pltpu.CompilerParams(
            collective_id=collective_id, has_side_effects=True, vmem_limit_bytes=62 * 2**20
        ),
        name="front",
    )(*inputs)


SPANS = ((0, 256), (256, 128))


def down_body(
    act_ref,
    w_hbm,
    gate_ref,
    hidden_hbm,
    slot_ref,
    came_hbm,
    dest_hbm,
    o_ref,
    arrived_ref,
    w_ref,
    hidden_ref,
    came_ref,
    dest_ref,
    p2,
    p1,
    pm,
    r1,
    fin,
    place,
    *rest,
):
    s1_send, s1_recv, s2_send, s2_recv, z_send, z_recv, x_send, x_recv, x_own, load_sem = rest[10:]
    turned, tf, zr, out_own, out_all = (rest[2 * k : 2 * k + 2] for k in range(5))
    me = coords()
    xc, kinds = ("x", "c"), ("ring", "ring")
    entered = greet(me, {"y": {1, 3}, "z": set(range(1, 8)), **partners(xc, kinds)})
    group = w_ref.shape[1] // 4
    loads = {}
    for k, step in enumerate((2, 1, 3, 0)):
        start = pl.multiple_of(lax.rem(me["y"] + step, 4) * group, 128)
        span = pl.ds(start, group)
        loads[step] = pltpu.make_async_copy(w_hbm.at[:, span], w_ref.at[:, span], load_sem.at[k])
        loads[step].start()
    late = [
        pltpu.make_async_copy(a, b, load_sem.at[4 + k])
        for k, (a, b) in enumerate(
            ((hidden_hbm, hidden_ref), (came_hbm, came_ref), (dest_hbm, dest_ref))
        )
    ]
    up, down = shifted(me, "y", 1), shifted(me, "y", -1)
    pair, odd = me["z"] // 2, lax.rem(me["z"], 2)
    wide = w_ref.shape[1] // 16
    n = wide // 4
    order = (2, 1, 3, 0)
    tokens = slot_ref.shape[1]
    copies, firsts, lasts, across = [], {}, {}, {}

    def product(p, step, k):
        there = lax.rem(me["y"] + step, 4)
        start = there * (4 * wide) + lax.rem(pair + k, 4) * wide
        rows = act_ref[pl.ds(*SPANS[p]), :]
        return dot_f32(rows, w_ref[:, pl.ds(pl.multiple_of(start, 128), wide)])

    def send(source, place, ss, rs, there):
        copy = remote(source, place, ss, rs, there)
        copy.start()
        copies.append(copy)
        return copy

    def halves(p):
        first, size = SPANS[p]
        return pl.ds(first, size // 2), pl.ds(first + size // 2, size // 2)

    def begin(p, k):
        low, high = halves(p)
        p2[k, pl.ds(*SPANS[p])] = product(p, 2, k).astype(p2.dtype)
        if (p, k) == (0, order[0]):
            entered()
        firsts[p, k] = (
            send(p2.at[k, low], r1.at[k, low], s1_send.at[p, k, 0], s1_recv.at[p, k, 0], up),
            send(p2.at[k, high], r1.at[k, high], s1_send.at[p, k, 1], s1_recv.at[p, k, 1], down),
        )

    def middle(p, k):
        low, high = halves(p)

        def on(source, side, piece, there):
            at = (p, k, side, 0 if piece is low else 1)
            return send(
                source.at[k, piece], fin.at[k, side, piece], s2_send.at[at], s2_recv.at[at], there
            )

        p1[k, pl.ds(*SPANS[p])] = product(p, 1, k).astype(p1.dtype)
        c = on(p1, 0, high, up)
        pm[k, pl.ds(*SPANS[p])] = product(p, 3, k).astype(pm.dtype)
        d = on(pm, 1, low, down)
        firsts[p, k][0].wait_recv()
        p1[k, low] = (p1[k, low].astype(jnp.float32) + r1[k, low].astype(jnp.float32)).astype(
            p1.dtype
        )
        e = on(p1, 0, low, up)
        firsts[p, k][1].wait_recv()
        pm[k, high] = (pm[k, high].astype(jnp.float32) + r1[k, high].astype(jnp.float32)).astype(
            pm.dtype
        )
        lasts[p, k] = (c, d, e, on(pm, 1, high, down))

    def end(p, k):
        whole = product(p, 0, k)
        for copy in lasts[p, k]:
            copy.wait_recv()
        span = pl.ds(*SPANS[p])
        whole = whole + (fin[k, 0, span].astype(jnp.float32) + fin[k, 1, span].astype(jnp.float32))
        whole = whole.T
        for e in range(2):
            part = whole[e * (wide // 2) : (e + 1) * (wide // 2)]
            turned[p][k, e] = part.astype(turned[p].dtype)
            if k == 0:
                tf[p][e] = part
        first = 2 * lax.rem(pair + k, 4)
        if k > 0:
            for e in range(2):
                slot = 2 * k + odd
                send(
                    turned[p].at[k, e],
                    zr[p].at[slot],
                    z_send.at[p, 2 * k + e],
                    z_recv.at[p, slot],
                    dict(me, z=first + e),
                )
        else:
            send(
                turned[p].at[0, 1 - odd],
                zr[p].at[odd],
                z_send.at[p, 0],
                z_recv.at[p, odd],
                dict(me, z=first + 1 - odd),
            )

    def total(p):
        found = tf[p][odd]
        for k in order:
            for e in range(2) if k > 0 else (0,):
                slot = 2 * k + e if k > 0 else 1 - odd
                remote(
                    zr[p].at[slot], zr[p].at[slot], z_send.at[p, 0], z_recv.at[p, slot], up
                ).wait_recv()
                found = found + zr[p][slot].astype(jnp.float32)
        found = found * gate_ref[:, pl.ds(*SPANS[p])]
        for h in range(2):
            out_own[p][h] = found[h * n : (h + 1) * n].astype(out_own[p].dtype)
            gather = Gather(
                me,
                out_own[p].at[h],
                lambda i, h=h: out_all[p].at[i, h],
                xc,
                kinds,
                h,
                (x_send, x_recv, x_own.at[2 * p + h]),
                8 * (2 * p + h),
            )
            gather.step(gather.plan.pop(0))
            across[p, h] = gather

    def one_hot(p):
        first, size = SPANS[p]
        slots = lax.broadcasted_iota(jnp.int32, (size, tokens), 0) + first
        for e in range(8):
            place[e, pl.ds(first, size)] = (
                (slot_ref[e : e + 1, :] == slots).astype(jnp.float32).astype(place.dtype)
            )

    def combine(p):
        run(across[p, 0], across[p, 1])
        for h in range(2):
            span = pl.ds(h * n, n)
            mixed = hidden_ref[span, :]
            for e in range(8):
                mixed = mixed + dot_f32(out_all[p][e, h], place[e, pl.ds(*SPANS[p])])
            hidden_ref[span, :] = mixed

    loads[2].wait()
    for k in order:
        begin(0, k)
    loads[1].wait()
    loads[3].wait()
    for load in late:
        load.start()
    for k in order:
        middle(0, k)
    for k in order:
        begin(1, k)
    loads[0].wait()
    end(0, 2)
    end(0, 1)
    one_hot(0)
    one_hot(1)
    end(0, 3)
    middle(1, 2)
    end(0, 0)
    for k in (1, 3, 0):
        middle(1, k)
    for load in late:
        load.wait()
    rep = lax.axis_index("rep")
    n_rep = dest_ref.shape[0]
    first, last = jnp.int32(n_rep), jnp.int32(-1)
    for source in range(n_rep):
        aimed = dest_ref[source] == rep
        first = jnp.where(aimed, jnp.minimum(first, source), first)
        last = jnp.where(aimed, source, last)
    for q, (source, there) in enumerate(((first, last >= 0), (last, last > first))):
        block = came_ref[jnp.clip(source, 0, n_rep - 1)].astype(jnp.float32)
        arrived_ref[0, q] = jnp.where(there, block, 0.0).astype(arrived_ref.dtype)
    end(1, 2)
    end(1, 1)
    total(0)
    end(1, 3)
    end(1, 0)
    combine(0)
    total(1)
    combine(1)
    o_ref[...] = hidden_ref[...].astype(o_ref.dtype)
    for copy in copies:
        copy.wait_send()
    for gather in across.values():
        gather.finish()


def down_and_scatter(act, w_down, gate, hidden, slots, came, mig_dest, collective_id):
    rows, depth = act.shape
    width = w_down.shape[1] // 16
    vmem = pl.BlockSpec(memory_space=pltpu.VMEM)
    hbm = pl.BlockSpec(memory_space=pltpu.HBM)
    kind = act.dtype
    return pl.pallas_call(
        down_body,
        out_shape=[
            jax.ShapeDtypeStruct(hidden.shape, kind),
            jax.ShapeDtypeStruct((1, IN_MOST, *came.shape[1:]), kind),
        ],
        in_specs=[vmem, hbm, vmem, hbm, vmem, hbm, hbm],
        out_specs=[vmem, vmem],
        scratch_shapes=[
            pltpu.VMEM(w_down.shape, kind),
            pltpu.VMEM(hidden.shape, hidden.dtype),
            pltpu.VMEM(came.shape, kind),
            pltpu.SMEM(mig_dest.shape, mig_dest.dtype),
            pltpu.VMEM((4, rows, width), kind),
            pltpu.VMEM((4, rows, width), kind),
            pltpu.VMEM((4, rows, width), kind),
            pltpu.VMEM((4, rows, width), kind),
            pltpu.VMEM((4, 2, rows, width), kind),
            pltpu.VMEM((8, rows, slots.shape[1]), kind),
            *[pltpu.VMEM((4, 2, width // 2, size), kind) for _, size in SPANS],
            *[pltpu.VMEM((2, width // 2, size), jnp.float32) for _, size in SPANS],
            *[pltpu.VMEM((8, width // 2, size), kind) for _, size in SPANS],
            *[pltpu.VMEM((2, width // 4, size), kind) for _, size in SPANS],
            *[pltpu.VMEM((8, 2, width // 4, size), kind) for _, size in SPANS],
            pltpu.SemaphoreType.DMA((2, 4, 2)),
            pltpu.SemaphoreType.DMA((2, 4, 2)),
            pltpu.SemaphoreType.DMA((2, 4, 2, 2)),
            pltpu.SemaphoreType.DMA((2, 4, 2, 2)),
            pltpu.SemaphoreType.DMA((2, 8)),
            pltpu.SemaphoreType.DMA((2, 8)),
            pltpu.SemaphoreType.DMA((32,)),
            pltpu.SemaphoreType.DMA((32,)),
            pltpu.SemaphoreType.DMA((4,)),
            pltpu.SemaphoreType.DMA((7,)),
        ],
        compiler_params=pltpu.CompilerParams(
            collective_id=collective_id, has_side_effects=True, vmem_limit_bytes=62 * 2**20
        ),
        name="down_scatter",
    )(act, w_down, gate, hidden, slots, came, mig_dest)


def contract_first(a, b, **kw):
    return lax.dot_general(
        a, b, (((0,), (0,)), ((), ())), preferred_element_type=jnp.float32, **kw
    )


def local(
    stream_in,
    query,
    new_kv,
    cache,
    precision,
    cache_scale,
    lengths,
    w_heads,
    norm_gain,
    w_router,
    expert_choice,
    w_in,
    w_down,
    mig_dest,
    mig_req,
    mig_blocks,
):
    tokens = stream_in.shape[0]
    capacity = tokens // 2
    ff = w_in.shape[3]
    choice = expert_choice.T
    rows = query.shape[0]
    u_all, extra_all, hidden, came, slots = front(
        [
            lengths,
            precision.T,
            jnp.transpose(cache_scale[..., 0], (1, 2, 0)).reshape(-1, rows),
            mig_req,
            mig_blocks,
            query,
            new_kv,
            cache,
            choice,
            w_heads.T,
            stream_in.T,
            norm_gain[None],
            w_router.T,
        ],
        capacity,
        1,
    )
    w_in, u_all = lax.optimization_barrier((w_in, u_all))
    sums = jnp.sum(extra_all, axis=0)
    inverse = lax.rsqrt(sums[0] / D + EPSILON)
    gate_of_slot = 1.0 / (1.0 + jnp.exp(-sums[1] * inverse))
    gate_up = contract_first(w_in[0].reshape(D, 2 * ff), u_all.reshape(D, capacity))
    gate_up = gate_up * inverse[None, :]
    act = (jax.nn.silu(gate_up[:ff]) * gate_up[ff:]).astype(jnp.bfloat16)
    mixed, arrived = down_and_scatter(
        act.T, w_down[0], gate_of_slot[None], hidden, slots, came, mig_dest, 2
    )
    return (mixed.T, arrived)


def solution(mesh):
    placed = (
        P(None, "rep"),
        P("rep", "hx"),
        P("rep", None, "hx"),
        P("rep", None, None, "hx"),
        P("rep", None),
        P("rep", None, None, "hx"),
        P("rep"),
        P("hx", "rep"),
        P("rep"),
        P("rep", None),
        P(),
        P("hx", None, None, "rep"),
        P("hx", "rep", None),
        P(),
        P(),
        P(),
    )
    return jax.shard_map(
        local,
        mesh=mesh,
        in_specs=placed,
        out_specs=(P(None, "rep"), P("rep", None, None, None, "hx")),
        check_vma=False,
    )
```

```python
import functools

import jax
import jax.numpy as jnp
from jax import lax
from jax.experimental import pallas as pl
from jax.experimental.pallas import tpu as pltpu
from jax.sharding import PartitionSpec as P

D = 6144
HEAD = 128
GROUP = 6
BLOCK_LEN = 32
IN_MOST = 2
CACHE = 128
EPSILON = 1e-05

SIZES = {"y": 4, "z": 8, "x": 4, "c": 2}
PLANE = ("y", "z")
CHIPS = ("x", "c")


def coords():
    rep = lax.axis_index("rep")
    hx = lax.axis_index("hx")
    return {"y": rep // 8, "z": lax.rem(rep, 8), "x": hx // 2, "c": lax.rem(hx, 2)}


def device_at(at):
    return {"rep": at["y"] * 8 + at["z"], "hx": at["x"] * 2 + at["c"]}


def shifted(at, dim, step):
    n = SIZES[dim]
    moved = dict(at)
    moved[dim] = lax.rem(at[dim] + (step % n), n)
    return moved


def index_in(at, dims):
    if "y" in dims:
        return at["y"] * 8 + at["z"]
    return at["x"] * 2 + at["c"]


TREES = {
    "ring": {
        2: {0: (1,)},
        4: {0: (1, -1), 1: (2,)},
        8: {0: (1, -1), 1: (2,), 2: (3,), 3: (4,), -1: (-2,), -2: (-3,)},
    },
    "two": {
        2: {0: (1,)},
        4: {0: (1, -1, 2)},
        8: {0: (1, -1, 2, -2), 2: (3, 4), -2: (-3,)},
    },
    "direct": {
        2: {0: (1,)},
        4: {0: (1, -1, 2)},
        8: {0: (1, -1, 2, -2, 3, -3, 4)},
    },
}


def tree_of(kind, n, flip):
    sign = -1 if flip % 2 and n > 2 else 1
    return {sign * o: tuple(sign * t for t in to) for o, to in TREES[kind][n].items()}


def places_of(tree):
    found = [0]
    for o in found:
        found += tree.get(o, ())
    return found


def depth_of(tree, o):
    if o == 0:
        return 0
    return 1 + depth_of(tree, next(p for p, to in tree.items() if o in to))


def gather_plan(dims, kinds, flip):
    na, nb = SIZES[dims[0]], SIZES[dims[1]]
    ta = tree_of(kinds[0], na, flip)
    events = []
    for oa in places_of(ta):
        tb = tree_of(kinds[1], nb, oa + flip)
        for ob in places_of(tb):
            sends = []
            if ob == 0:
                sends += [(t, 0) for t in ta.get(oa, ())]
            sends += [(oa, t) for t in tb.get(ob, ())]
            cost = 3 * (depth_of(ta, oa) + depth_of(tb, ob)) + abs(oa) + abs(ob)
            events.append((cost, oa, ob, sends))
    return sorted(events, key=lambda e: e[0])


def partners(dims, kinds):
    found = {}
    for dim, kind in zip(dims, kinds):
        steps = found.setdefault(dim, set())
        for o, to in TREES[kind][SIZES[dim]].items():
            for t in to:
                steps |= {(t - o) % SIZES[dim], (o - t) % SIZES[dim]}
    return found


def greet(me, steps):
    barrier = pltpu.get_barrier_semaphore()
    count = 0
    for dim in sorted(steps):
        for step in sorted(steps[dim]):
            pl.semaphore_signal(
                barrier,
                inc=1,
                device_id=device_at(shifted(me, dim, step)),
                device_id_type=pl.DeviceIdType.MESH,
            )
            count += 1
    return lambda: pl.semaphore_wait(barrier, count)


def remote(source, place, send_sem, recv_sem, there):
    return pltpu.make_async_remote_copy(
        src_ref=source,
        dst_ref=place,
        send_sem=send_sem,
        recv_sem=recv_sem,
        device_id=device_at(there),
        device_id_type=pl.DeviceIdType.MESH,
    )


class Gather:
    def __init__(self, me, source, place, dims, kinds, flip, sems, base):
        self.me, self.source, self.place = me, source, place
        self.dims, self.kinds, self.flip = dims, kinds, flip
        self.send_sem, self.recv_sem, self.own_sem = sems
        self.plan = gather_plan(dims, kinds, flip)
        self.slots = {(oa, ob): base + k for k, (_, oa, ob, _) in enumerate(self.plan)}
        self.copies = []

    def at(self, oa, ob):
        origin = shifted(shifted(self.me, self.dims[0], -oa), self.dims[1], -ob)
        return self.place(index_in(origin, self.dims))

    def step(self, event):
        _, oa, ob, sends = event
        place = self.at(oa, ob)
        source = place
        if (oa, ob) == (0, 0):
            source = self.source
        else:
            slot = self.slots[oa, ob]
            near = shifted(self.me, self.dims[0], 1)
            remote(place, place, self.send_sem.at[0], self.recv_sem.at[slot], near).wait_recv()
        for to in sends:
            there = shifted(shifted(self.me, self.dims[0], to[0] - oa), self.dims[1], to[1] - ob)
            slot = self.slots[to]
            copy = remote(source, place, self.send_sem.at[slot], self.recv_sem.at[slot], there)
            copy.start()
            self.copies.append(copy)
        if (oa, ob) == (0, 0):
            self.own = pltpu.make_async_copy(source, place, self.own_sem)
            self.own.start()

    def finish(self):
        for copy in self.copies:
            copy.wait_send()


def run(*gathers):
    todo = [(e[0], n, e) for n, g in enumerate(gathers) for e in g.plan]
    for _, n, event in sorted(todo, key=lambda e: e[:2]):
        gathers[n].step(event)
    for g in gathers:
        g.own.wait()


def dot_f32(a, b):
    return jnp.dot(a, b, preferred_element_type=jnp.float32)


def split_three(x):
    high = x.astype(jnp.bfloat16)
    rest = x - high.astype(jnp.float32)
    middle = rest.astype(jnp.bfloat16)
    low = (rest - middle.astype(jnp.float32)).astype(jnp.bfloat16)
    return high, middle, low


def attend(scalars, q_ref, new_ref, cache_ref, left_ref, right_ref, queries, scores, weights):
    lengths, factor = scalars
    rows = q_ref.shape[0]
    scale = HEAD ** (-0.5)
    queries[...] = jnp.zeros_like(queries)
    for g in range(GROUP):
        queries[:, g, :] = q_ref[:, g * HEAD : (g + 1) * HEAD].astype(jnp.float32)
    lane = lax.broadcasted_iota(jnp.int32, (8, CACHE), 1)

    def along(j, r):
        row = jnp.full((8, CACHE), factor(j, 3, r))
        for b in (2, 1, 0):
            row = jnp.where(lane < (b + 1) * BLOCK_LEN, factor(j, b, r), row)
        return row

    for r in range(rows):
        raw = lax.dot_general(
            queries[r].astype(jnp.bfloat16),
            cache_ref[r, 0],
            (((1,), (1,)), ((), ())),
            preferred_element_type=jnp.float32,
        )
        scores[r] = jnp.where(lane < lengths[r], raw * along(0, r) * scale, -jnp.inf)
        weights[r] = along(1, r)
    fresh = new_ref[...].astype(jnp.float32)
    own = jnp.sum(queries[...] * fresh[:, 0:1, :], axis=2, keepdims=True) * scale
    s = scores[...]
    top = jnp.maximum(jnp.max(s, axis=2, keepdims=True), own)
    s = jnp.exp(s - top)
    own = jnp.exp(own - top)
    total = jnp.sum(s, axis=2, keepdims=True) + own
    weights[...] = s / total * weights[...]
    own = (own / total).astype(jnp.bfloat16).astype(jnp.float32) * fresh[:, 1:2, :]
    for r in range(rows):
        scores[r] = dot_f32(weights[r].astype(jnp.bfloat16), cache_ref[r, 1])
    scores[...] = scores[...] + own
    for g in range(GROUP):
        ref = left_ref if g < GROUP // 2 else right_ref
        at = g % (GROUP // 2)
        ref[:, at * HEAD : (at + 1) * HEAD] = scores[:, g, :].astype(ref.dtype)


def hand_off(cache_ref, factor, request, blocks, going_ref):
    for j in range(2):
        for b in range(CACHE // BLOCK_LEN):
            span = pl.ds(b * BLOCK_LEN, BLOCK_LEN)
            levels = cache_ref[request, j, span, :].astype(jnp.float32)
            going_ref[j, span, :] = jnp.where(
                b < blocks, levels * factor(j, b, request), 0.0
            ).astype(going_ref.dtype)


def route(choice_ref, slot_ref, pick_ref, expert):
    tokens = choice_ref.shape[1]
    experts = slot_ref.shape[0]
    ids = lax.broadcasted_iota(jnp.int32, (experts, tokens), 0)
    order = lax.broadcasted_iota(jnp.int32, (experts, tokens), 1)
    named = (choice_ref[0:1, :] == ids) | (choice_ref[1:2, :] == ids)
    count = named.astype(jnp.int32)
    step = 1
    while step < tokens:
        count = count + jnp.where(order >= step, pltpu.roll(count, step, 1), 0)
        step *= 2
    slots = jnp.where(named, count - 1, -1)
    slot_ref[...] = slots
    mine = jnp.sum(jnp.where(ids == expert, slots, 0).astype(jnp.float32).T, axis=1, keepdims=True)
    capacity = pick_ref.shape[1]
    across = lax.broadcasted_iota(jnp.int32, (tokens, capacity), 1).astype(jnp.float32)
    pick_ref[...] = (mine == across).astype(jnp.float32).astype(pick_ref.dtype)


def front_items():
    zy, yz, xc = ("z", "y"), ("y", "z"), ("x", "c")
    two, ring = ("two", "two"), ("ring", "ring")
    return {
        "left": (zy, two, 0),
        "right": (yz, two, 1),
        **{"part%d" % n: (xc, ring, n) for n in range(4)},
        "going0": (zy, ring, 0),
        "going1": (yz, ring, 1),
        **{"rows%d" % n: (zy if n % 2 == 0 else yz, ring, n // 2 + n % 2) for n in range(4)},
        "extra": (yz, ring, 0),
    }


PIECES = ((0, 64), (64, 32), (96, 48), (144, 48))
PARTS = ((0, 48), (48, 48), (96, 48), (144, 48))


def members(item):
    return SIZES[item[0][0]] * SIZES[item[0][1]]


def front_body(*refs):
    hbm, outs, scratch = refs[:13], refs[13:18], refs[18:]
    u_ref, factor_ref, hidden_ref, came_ref, slot_ref = outs
    local_refs, scratch = scratch[:13], scratch[13:]
    (
        lengths,
        precision,
        scales,
        mig_req,
        mig_blocks,
        q_ref,
        new_ref,
        cache_ref,
        choice_ref,
        w_ref,
        stream_ref,
        gain_ref,
        router_ref,
    ) = local_refs
    (
        left_ref,
        right_ref,
        going_ref,
        pick_ref,
        queries,
        scores,
        weights,
        left_all,
        right_all,
        part_own,
        part_all,
        rows_own,
        extra_own,
        extra_all,
        send_sem,
        recv_sem,
        own_sem,
        load_sem,
    ) = scratch
    me = coords()
    items = front_items()
    greeted = {}
    for dims, kinds, _ in items.values():
        for dim, steps in partners(dims, kinds).items():
            greeted.setdefault(dim, set()).update(steps)
    entered = greet(me, greeted)
    loads = [
        pltpu.make_async_copy(a, b, load_sem.at[k])
        for k, (a, b) in enumerate(zip(hbm, local_refs))
    ]
    for load in loads:
        load.start()

    def factor(j, b, r):
        return jnp.where(precision[b, r] == 1, scales[4 * j + b, r], 1.0)

    for load in loads[:8]:
        load.wait()
    attend(
        (lengths, factor), q_ref, new_ref, cache_ref, left_ref, right_ref, queries, scores, weights
    )
    rep = lax.axis_index("rep")
    entered()
    refs = {
        "left": (left_ref, lambda i: left_all.at[i]),
        "right": (right_ref, lambda i: right_all.at[i]),
        **{
            "part%d" % n: (
                part_own.at[pl.ds(*piece)],
                lambda i, piece=piece: part_all.at[i, pl.ds(*piece)],
            )
            for n, piece in enumerate(PARTS)
        },
        "going0": (going_ref.at[0], lambda i: came_ref.at[i, 0]),
        "going1": (going_ref.at[1], lambda i: came_ref.at[i, 1]),
        **{
            "rows%d" % n: (
                rows_own.at[pl.ds(*piece)],
                lambda i, piece=piece: u_ref.at[i, pl.ds(*piece)],
            )
            for n, piece in enumerate(PIECES)
        },
        "extra": (extra_own, lambda i: extra_all.at[i]),
    }
    g, base = {}, 0
    for n, (name, (dims, kinds, flip)) in enumerate(items.items()):
        sems = (send_sem, recv_sem, own_sem.at[n])
        g[name] = Gather(me, *refs[name], dims, kinds, flip, sems, base)
        base += members(items[name])
    moving = sorted(
        [(e[0], n, e) for n in (0, 1) for e in g["going%d" % n].plan], key=lambda e: e[:2]
    )

    def move(depth):
        while moving and moving[0][0] <= depth:
            _, n, event = moving.pop(0)
            g["going%d" % n].step(event)

    todo = sorted(
        [(e[0], n, e) for n, k in enumerate(("left", "right")) for e in g[k].plan],
        key=lambda e: e[:2],
    )
    for k, (cost, n, event) in enumerate(todo):
        if k == 2:
            hand_off(cache_ref, factor, mig_req[rep], mig_blocks[rep], going_ref)
            move(0)
            for load in loads[8:]:
                load.wait()
            route(choice_ref, slot_ref, pick_ref, lax.axis_index("hx"))
        g[("left", "right")[n]].step(event)
    for k in ("left", "right"):
        g[k].own.wait()

    split = left_ref.shape[1]
    tokens = stream_ref.shape[1]
    transposed = (((1,), (1,)), ((), ()))
    half = stream_ref.shape[0] // 2
    for n in range(2):
        span = pl.ds(n * half, half)
        part = lax.dot_general(
            w_ref[span, :split],
            left_all[...].reshape(tokens, split),
            transposed,
            preferred_element_type=jnp.float32,
        ) + lax.dot_general(
            w_ref[span, split:],
            right_all[...].reshape(tokens, split),
            transposed,
            preferred_element_type=jnp.float32,
        )
        part_own[span, :] = part.astype(part_own.dtype)
        for k in (2 * n, 2 * n + 1):
            g["part%d" % k].step(g["part%d" % k].plan.pop(0))
    move(4)

    def early(n):
        names = ["part%d" % k for k in (2 * n, 2 * n + 1)]
        found = sorted([(e[0], k, e) for k in names for e in g[k].plan], key=lambda e: e[:2])
        for _, k, event in found:
            g[k].step(event)
        for k in names:
            g[k].own.wait()
        move(8)

    gain = jnp.broadcast_to(gain_ref[...], (8, gain_ref.shape[1])).T[:, :1]
    squares = jnp.zeros((1, tokens), jnp.float32)
    logits = jnp.zeros((router_ref.shape[0], tokens), jnp.float32)
    for n in range(2):
        span = pl.ds(n * half, half)
        early(n)
        hidden = stream_ref[span, :].astype(jnp.float32)
        for e in range(part_all.shape[0]):
            hidden = hidden + part_all[e, span, :].astype(jnp.float32)
        hidden_ref[span, :] = hidden
        gained = hidden * gain[n * half : (n + 1) * half]
        rows_own[span, :] = dot_f32(gained.astype(jnp.bfloat16), pick_ref[...]).astype(
            rows_own.dtype
        )
        for k in (2 * n, 2 * n + 1):
            g["rows%d" % k].step(g["rows%d" % k].plan.pop(0))
        squares = squares + jnp.sum(hidden * hidden, axis=0, keepdims=True)
        logits = logits + jnp.dot(
            router_ref[:, n * half : (n + 1) * half].astype(jnp.float32),
            gained,
            precision=lax.Precision.HIGHEST,
            preferred_element_type=jnp.float32,
        )
    ids = lax.broadcasted_iota(jnp.int32, logits.shape, 0)
    choice = choice_ref[...]
    first = jnp.sum(jnp.where(choice[0:1] == ids, logits, 0.0), axis=0, keepdims=True)
    second = jnp.sum(jnp.where(choice[1:2] == ids, logits, 0.0), axis=0, keepdims=True)
    ahead = jnp.where(choice[0:1] == lax.axis_index("hx"), first - second, second - first)
    terms = jnp.concatenate(
        [t.astype(jnp.float32) for t in split_three(squares) + split_three(ahead)]
        + [jnp.zeros((2, tokens), jnp.float32)],
        axis=0,
    ).astype(jnp.bfloat16)
    chosen = dot_f32(terms, pick_ref[...])
    extra_own[...] = jnp.concatenate(
        [
            chosen[0:1] + chosen[1:2] + chosen[2:3],
            chosen[3:4] + chosen[4:5] + chosen[5:6],
            chosen[2:8] * 0.0,
        ],
        axis=0,
    )
    move(11)
    last = ("rows0", "rows1", "rows2", "rows3", "extra")
    todo = sorted(
        [(e[0], n, e) for n, k in enumerate(last) for e in g[k].plan],
        key=lambda e: e[:2],
    )
    for cost, n, event in todo:
        if cost > 8:
            move(cost + 2)
        g[last[n]].step(event)
    move(10**6)
    for k in (*last, "going0", "going1"):
        g[k].own.wait()
    sums = jnp.sum(extra_all[...], axis=0)
    inverse = lax.rsqrt(sums[0:1] / D + EPSILON)
    gate = 1.0 / (1.0 + jnp.exp(-sums[1:2] * inverse))
    factor_ref[...] = jnp.concatenate([inverse, gate, sums[2:8] * 0.0], axis=0)
    for k in g:
        g[k].finish()


def front(inputs, capacity, collective_id):
    query, stream = inputs[5], inputs[10]
    rows, wide = query.shape
    split = wide // 2
    mine, tokens = stream.shape
    half = mine // 2
    kind = query.dtype
    going = inputs[7].shape[1:]
    vmem = pl.BlockSpec(memory_space=pltpu.VMEM)
    anywhere = pl.BlockSpec(memory_space=pl.ANY)
    items = front_items()
    total = sum(members(item) for item in items.values())
    spaces = [pltpu.SMEM] * 5 + [pltpu.VMEM] * 8
    return pl.pallas_call(
        front_body,
        out_shape=[
            jax.ShapeDtypeStruct((32, mine, capacity), kind),
            jax.ShapeDtypeStruct((8, capacity), jnp.float32),
            jax.ShapeDtypeStruct((mine, tokens), jnp.float32),
            jax.ShapeDtypeStruct((32, *going), kind),
            jax.ShapeDtypeStruct((8, tokens), jnp.int32),
        ],
        in_specs=[pl.BlockSpec(memory_space=pltpu.HBM)] * 13,
        out_specs=[anywhere, vmem, vmem, anywhere, vmem],
        scratch_shapes=[space(x.shape, x.dtype) for space, x in zip(spaces, inputs)]
        + [
            pltpu.VMEM((rows, split), kind),
            pltpu.VMEM((rows, split), kind),
            pltpu.VMEM(going, kind),
            pltpu.VMEM((tokens, capacity), kind),
            pltpu.VMEM((rows, 8, HEAD), jnp.float32),
            pltpu.VMEM((rows, 8, HEAD), jnp.float32),
            pltpu.VMEM((rows, 8, HEAD), jnp.float32),
            pltpu.VMEM((32, rows, split), kind),
            pltpu.VMEM((32, rows, split), kind),
            pltpu.VMEM((mine, tokens), kind),
            pltpu.VMEM((8, mine, tokens), kind),
            pltpu.VMEM((mine, capacity), kind),
            pltpu.VMEM((8, capacity), jnp.float32),
            pltpu.VMEM((32, 8, capacity), jnp.float32),
            pltpu.SemaphoreType.DMA((total,)),
            pltpu.SemaphoreType.DMA((total,)),
            pltpu.SemaphoreType.DMA((len(items),)),
            pltpu.SemaphoreType.DMA((13,)),
        ],
        compiler_params=pltpu.CompilerParams(
            collective_id=collective_id, has_side_effects=True, vmem_limit_bytes=62 * 2**20
        ),
        name="front",
    )(*inputs)


SPANS = ((0, 256), (256, 128))


def down_body(
    raw_ref,
    w_hbm,
    factor_ref,
    hidden_hbm,
    slot_ref,
    came_hbm,
    dest_hbm,
    o_ref,
    arrived_ref,
    w_ref,
    hidden_ref,
    came_ref,
    dest_ref,
    act_ref,
    p2,
    p1,
    pm,
    r1,
    fin,
    place,
    *rest,
):
    s1_send, s1_recv, s2_send, s2_recv, z_send, z_recv, x_send, x_recv, x_own, load_sem = rest[10:]
    turned, tf, zr, out_own, out_all = (rest[2 * k : 2 * k + 2] for k in range(5))
    me = coords()
    xc, routes = ("x", "c"), (("ring", "ring"), ("two", "ring"))
    entered = greet(me, {"y": {1, 3}, "z": set(range(1, 8)), **partners(xc, routes[1])})
    group = w_ref.shape[1] // 4
    loads = {}
    for k, step in enumerate((2, 1, 3, 0)):
        start = pl.multiple_of(lax.rem(me["y"] + step, 4) * group, 128)
        span = pl.ds(start, group)
        loads[step] = pltpu.make_async_copy(w_hbm.at[:, span], w_ref.at[:, span], load_sem.at[k])
        loads[step].start()
    late = [
        pltpu.make_async_copy(a, b, load_sem.at[4 + k])
        for k, (a, b) in enumerate(
            ((hidden_hbm, hidden_ref), (came_hbm, came_ref), (dest_hbm, dest_ref))
        )
    ]
    up, down = shifted(me, "y", 1), shifted(me, "y", -1)
    pair, odd = me["z"] // 2, lax.rem(me["z"], 2)
    wide = w_ref.shape[1] // 16
    n = wide // 4
    order = (2, 1, 3, 0)
    tokens = slot_ref.shape[1]
    copies, firsts, lasts, across = [], {}, {}, {}

    def product(p, step, k):
        there = lax.rem(me["y"] + step, 4)
        start = there * (4 * wide) + lax.rem(pair + k, 4) * wide
        rows = act_ref[pl.ds(*SPANS[p]), :]
        return dot_f32(rows, w_ref[:, pl.ds(pl.multiple_of(start, 128), wide)])

    def send(source, place, ss, rs, there):
        copy = remote(source, place, ss, rs, there)
        copy.start()
        copies.append(copy)
        return copy

    def halves(p):
        first, size = SPANS[p]
        return pl.ds(first, size // 2), pl.ds(first + size // 2, size // 2)

    def begin(p, k):
        low, high = halves(p)
        p2[k, pl.ds(*SPANS[p])] = product(p, 2, k).astype(p2.dtype)
        if (p, k) == (0, order[0]):
            entered()
        firsts[p, k] = (
            send(p2.at[k, low], r1.at[k, low], s1_send.at[p, k, 0], s1_recv.at[p, k, 0], up),
            send(p2.at[k, high], r1.at[k, high], s1_send.at[p, k, 1], s1_recv.at[p, k, 1], down),
        )

    def middle(p, k):
        low, high = halves(p)

        def on(source, side, piece, there):
            at = (p, k, side, 0 if piece is low else 1)
            return send(
                source.at[k, piece], fin.at[k, side, piece], s2_send.at[at], s2_recv.at[at], there
            )

        p1[k, pl.ds(*SPANS[p])] = product(p, 1, k).astype(p1.dtype)
        c = on(p1, 0, high, up)
        pm[k, pl.ds(*SPANS[p])] = product(p, 3, k).astype(pm.dtype)
        d = on(pm, 1, low, down)
        firsts[p, k][0].wait_recv()
        p1[k, low] = (p1[k, low].astype(jnp.float32) + r1[k, low].astype(jnp.float32)).astype(
            p1.dtype
        )
        e = on(p1, 0, low, up)
        firsts[p, k][1].wait_recv()
        pm[k, high] = (pm[k, high].astype(jnp.float32) + r1[k, high].astype(jnp.float32)).astype(
            pm.dtype
        )
        lasts[p, k] = (c, d, e, on(pm, 1, high, down))

    def end(p, k):
        whole = product(p, 0, k)
        for copy in lasts[p, k]:
            copy.wait_recv()
        span = pl.ds(*SPANS[p])
        whole = whole + (fin[k, 0, span].astype(jnp.float32) + fin[k, 1, span].astype(jnp.float32))
        whole = whole.T
        for e in range(2):
            part = whole[e * (wide // 2) : (e + 1) * (wide // 2)]
            turned[p][k, e] = part.astype(turned[p].dtype)
            if k == 0:
                tf[p][e] = part
        first = 2 * lax.rem(pair + k, 4)
        if k > 0:
            for e in range(2):
                slot = 2 * k + odd
                send(
                    turned[p].at[k, e],
                    zr[p].at[slot],
                    z_send.at[p, 2 * k + e],
                    z_recv.at[p, slot],
                    dict(me, z=first + e),
                )
        else:
            send(
                turned[p].at[0, 1 - odd],
                zr[p].at[odd],
                z_send.at[p, 0],
                z_recv.at[p, odd],
                dict(me, z=first + 1 - odd),
            )

    def total(p):
        found = tf[p][odd]
        for k in order:
            for e in range(2) if k > 0 else (0,):
                slot = 2 * k + e if k > 0 else 1 - odd
                remote(
                    zr[p].at[slot], zr[p].at[slot], z_send.at[p, 0], z_recv.at[p, slot], up
                ).wait_recv()
                found = found + zr[p][slot].astype(jnp.float32)
        found = found * factor_ref[1:2, pl.ds(*SPANS[p])]
        for h in range(2):
            out_own[p][h] = found[h * n : (h + 1) * n].astype(out_own[p].dtype)
            gather = Gather(
                me,
                out_own[p].at[h],
                lambda i, h=h: out_all[p].at[i, h],
                xc,
                routes[p],
                h,
                (x_send, x_recv, x_own.at[2 * p + h]),
                8 * (2 * p + h),
            )
            gather.step(gather.plan.pop(0))
            across[p, h] = gather

    def one_hot(p):
        first, size = SPANS[p]
        slots = lax.broadcasted_iota(jnp.int32, (size, tokens), 0) + first
        for e in range(8):
            place[e, pl.ds(first, size)] = (
                (slot_ref[e : e + 1, :] == slots).astype(jnp.float32).astype(place.dtype)
            )

    def combine(p):
        run(across[p, 0], across[p, 1])
        for h in range(2):
            span = pl.ds(h * n, n)
            mixed = hidden_ref[span, :]
            for e in range(8):
                mixed = mixed + dot_f32(out_all[p][e, h], place[e, pl.ds(*SPANS[p])])
            hidden_ref[span, :] = mixed

    inverse = jnp.broadcast_to(factor_ref[0:1, :], factor_ref.shape).T[:, :1]
    depth = act_ref.shape[1]
    gate = raw_ref[:, :depth] * inverse
    act = gate * (1.0 / (1.0 + jnp.exp(-gate))) * (raw_ref[:, depth:] * inverse)
    act_ref[...] = act.astype(act_ref.dtype)
    loads[2].wait()
    for k in order:
        begin(0, k)
    loads[1].wait()
    loads[3].wait()
    for load in late:
        load.start()
    for k in order:
        middle(0, k)
    for k in order:
        begin(1, k)
    loads[0].wait()
    end(0, 2)
    end(0, 1)
    one_hot(0)
    one_hot(1)
    end(0, 3)
    middle(1, 2)
    end(0, 0)
    for k in (1, 3, 0):
        middle(1, k)
    for load in late:
        load.wait()
    rep = lax.axis_index("rep")
    n_rep = dest_ref.shape[0]
    first, last = jnp.int32(n_rep), jnp.int32(-1)
    for source in range(n_rep):
        aimed = dest_ref[source] == rep
        first = jnp.where(aimed, jnp.minimum(first, source), first)
        last = jnp.where(aimed, source, last)
    for q, (source, there) in enumerate(((first, last >= 0), (last, last > first))):
        block = came_ref[jnp.clip(source, 0, n_rep - 1)].astype(jnp.float32)
        arrived_ref[0, q] = jnp.where(there, block, 0.0).astype(arrived_ref.dtype)
    end(1, 2)
    end(1, 1)
    total(0)
    end(1, 3)
    end(1, 0)
    combine(0)
    total(1)
    combine(1)
    o_ref[...] = hidden_ref[...].astype(o_ref.dtype)
    for copy in copies:
        copy.wait_send()
    for gather in across.values():
        gather.finish()


def down_and_scatter(raw, w_down, factors, hidden, slots, came, mig_dest, collective_id):
    rows, depth = raw.shape[0], w_down.shape[0]
    width = w_down.shape[1] // 16
    vmem = pl.BlockSpec(memory_space=pltpu.VMEM)
    hbm = pl.BlockSpec(memory_space=pltpu.HBM)
    kind = w_down.dtype
    return pl.pallas_call(
        down_body,
        out_shape=[
            jax.ShapeDtypeStruct(hidden.shape, kind),
            jax.ShapeDtypeStruct((1, IN_MOST, *came.shape[1:]), kind),
        ],
        in_specs=[vmem, hbm, vmem, hbm, vmem, hbm, hbm],
        out_specs=[vmem, vmem],
        scratch_shapes=[
            pltpu.VMEM(w_down.shape, kind),
            pltpu.VMEM(hidden.shape, hidden.dtype),
            pltpu.VMEM(came.shape, kind),
            pltpu.SMEM(mig_dest.shape, mig_dest.dtype),
            pltpu.VMEM((rows, depth), kind),
            pltpu.VMEM((4, rows, width), kind),
            pltpu.VMEM((4, rows, width), kind),
            pltpu.VMEM((4, rows, width), kind),
            pltpu.VMEM((4, rows, width), kind),
            pltpu.VMEM((4, 2, rows, width), kind),
            pltpu.VMEM((8, rows, slots.shape[1]), kind),
            *[pltpu.VMEM((4, 2, width // 2, size), kind) for _, size in SPANS],
            *[pltpu.VMEM((2, width // 2, size), jnp.float32) for _, size in SPANS],
            *[pltpu.VMEM((8, width // 2, size), kind) for _, size in SPANS],
            *[pltpu.VMEM((2, width // 4, size), kind) for _, size in SPANS],
            *[pltpu.VMEM((8, 2, width // 4, size), kind) for _, size in SPANS],
            pltpu.SemaphoreType.DMA((2, 4, 2)),
            pltpu.SemaphoreType.DMA((2, 4, 2)),
            pltpu.SemaphoreType.DMA((2, 4, 2, 2)),
            pltpu.SemaphoreType.DMA((2, 4, 2, 2)),
            pltpu.SemaphoreType.DMA((2, 8)),
            pltpu.SemaphoreType.DMA((2, 8)),
            pltpu.SemaphoreType.DMA((32,)),
            pltpu.SemaphoreType.DMA((32,)),
            pltpu.SemaphoreType.DMA((4,)),
            pltpu.SemaphoreType.DMA((7,)),
        ],
        compiler_params=pltpu.CompilerParams(
            collective_id=collective_id, has_side_effects=True, vmem_limit_bytes=62 * 2**20
        ),
        name="down_scatter",
    )(raw, w_down, factors, hidden, slots, came, mig_dest)


def finish_body(mixed_ref, arrived_ref, mixed_out, arrived_out):
    mixed_out[...] = mixed_ref[...]
    arrived_out[...] = arrived_ref[...]


def finish(mixed, arrived):
    vmem = pl.BlockSpec(memory_space=pltpu.VMEM)
    return pl.pallas_call(
        finish_body,
        out_shape=[jax.ShapeDtypeStruct(x.shape, x.dtype) for x in (mixed, arrived)],
        in_specs=[vmem] * 2,
        out_specs=[vmem] * 2,
        name="finish",
    )(mixed, arrived)


def contract_first(a, b, **kw):
    return lax.dot_general(
        a, b, (((0,), (0,)), ((), ())), preferred_element_type=jnp.float32, **kw
    )


def local(
    stream_in,
    query,
    new_kv,
    cache,
    precision,
    cache_scale,
    lengths,
    w_heads,
    norm_gain,
    w_router,
    expert_choice,
    w_in,
    w_down,
    mig_dest,
    mig_req,
    mig_blocks,
):
    tokens = stream_in.shape[0]
    capacity = tokens // 2
    ff = w_in.shape[3]
    choice = expert_choice.T
    rows = query.shape[0]
    u_all, factors, hidden, came, slots = front(
        [
            lengths,
            precision.T,
            jnp.transpose(cache_scale[..., 0], (1, 2, 0)).reshape(-1, rows),
            mig_req,
            mig_blocks,
            query,
            new_kv,
            cache,
            choice,
            w_heads.T,
            stream_in.T,
            norm_gain[None],
            w_router.T,
        ],
        capacity,
        1,
    )
    w_in, u_all = lax.optimization_barrier((w_in, u_all))
    gate_up = contract_first(u_all.reshape(D, capacity), w_in[0].reshape(D, 2 * ff))
    mixed, arrived = down_and_scatter(
        gate_up, w_down[0], factors, hidden, slots, came, mig_dest, 2
    )
    mixed, arrived = finish(mixed, arrived)
    return (mixed.T, arrived)


def solution(mesh):
    placed = (
        P(None, "rep"),
        P("rep", "hx"),
        P("rep", None, "hx"),
        P("rep", None, None, "hx"),
        P("rep", None),
        P("rep", None, None, "hx"),
        P("rep"),
        P("hx", "rep"),
        P("rep"),
        P("rep", None),
        P(),
        P("hx", None, None, "rep"),
        P("hx", "rep", None),
        P(),
        P(),
        P(),
    )
    return jax.shard_map(
        local,
        mesh=mesh,
        in_specs=placed,
        out_specs=(P(None, "rep"), P("rep", None, None, None, "hx")),
        check_vma=False,
    )
```

```python
import functools

import jax
import jax.numpy as jnp
from jax import lax
from jax.experimental import pallas as pl
from jax.experimental.pallas import tpu as pltpu
from jax.sharding import PartitionSpec as P

D = 6144
HEAD = 128
GROUP = 6
BLOCK_LEN = 32
IN_MOST = 2
CACHE = 128
EPSILON = 1e-05

SIZES = {"y": 4, "z": 8, "x": 4, "c": 2}
PLANE = ("y", "z")
CHIPS = ("x", "c")


def coords():
    rep = lax.axis_index("rep")
    hx = lax.axis_index("hx")
    return {"y": rep // 8, "z": lax.rem(rep, 8), "x": hx // 2, "c": lax.rem(hx, 2)}


def device_at(at):
    return {"rep": at["y"] * 8 + at["z"], "hx": at["x"] * 2 + at["c"]}


def shifted(at, dim, step):
    n = SIZES[dim]
    moved = dict(at)
    moved[dim] = lax.rem(at[dim] + (step % n), n)
    return moved


def index_in(at, dims):
    if "y" in dims:
        return at["y"] * 8 + at["z"]
    return at["x"] * 2 + at["c"]


TREES = {
    "ring": {
        2: {0: (1,)},
        4: {0: (1, -1), 1: (2,)},
        8: {0: (1, -1), 1: (2,), 2: (3,), 3: (4,), -1: (-2,), -2: (-3,)},
    },
    "two": {
        2: {0: (1,)},
        4: {0: (1, -1, 2)},
        8: {0: (1, -1, 2, -2), 2: (3, 4), -2: (-3,)},
    },
    "direct": {
        2: {0: (1,)},
        4: {0: (1, -1, 2)},
        8: {0: (1, -1, 2, -2, 3, -3, 4)},
    },
}


def tree_of(kind, n, flip):
    sign = -1 if flip % 2 and n > 2 else 1
    return {sign * o: tuple(sign * t for t in to) for o, to in TREES[kind][n].items()}


def places_of(tree):
    found = [0]
    for o in found:
        found += tree.get(o, ())
    return found


def depth_of(tree, o):
    if o == 0:
        return 0
    return 1 + depth_of(tree, next(p for p, to in tree.items() if o in to))


def gather_plan(dims, kinds, flip):
    na, nb = SIZES[dims[0]], SIZES[dims[1]]
    ta = tree_of(kinds[0], na, flip)
    events = []
    for oa in places_of(ta):
        tb = tree_of(kinds[1], nb, oa + flip)
        for ob in places_of(tb):
            sends = []
            if ob == 0:
                sends += [(t, 0) for t in ta.get(oa, ())]
            sends += [(oa, t) for t in tb.get(ob, ())]
            cost = 3 * (depth_of(ta, oa) + depth_of(tb, ob)) + abs(oa) + abs(ob)
            events.append((cost, oa, ob, sends))
    return sorted(events, key=lambda e: e[0])


def partners(dims, kinds):
    found = {}
    for dim, kind in zip(dims, kinds):
        steps = found.setdefault(dim, set())
        for o, to in TREES[kind][SIZES[dim]].items():
            for t in to:
                steps |= {(t - o) % SIZES[dim], (o - t) % SIZES[dim]}
    return found


def greet(me, steps):
    barrier = pltpu.get_barrier_semaphore()
    count = 0
    for dim in sorted(steps):
        for step in sorted(steps[dim]):
            pl.semaphore_signal(
                barrier,
                inc=1,
                device_id=device_at(shifted(me, dim, step)),
                device_id_type=pl.DeviceIdType.MESH,
            )
            count += 1
    return lambda: pl.semaphore_wait(barrier, count)


def remote(source, place, send_sem, recv_sem, there):
    return pltpu.make_async_remote_copy(
        src_ref=source,
        dst_ref=place,
        send_sem=send_sem,
        recv_sem=recv_sem,
        device_id=device_at(there),
        device_id_type=pl.DeviceIdType.MESH,
    )


class Gather:
    def __init__(self, me, source, place, dims, kinds, flip, sems, base):
        self.me, self.source, self.place = me, source, place
        self.dims, self.kinds, self.flip = dims, kinds, flip
        self.send_sem, self.recv_sem, self.own_sem = sems
        self.plan = gather_plan(dims, kinds, flip)
        self.slots = {(oa, ob): base + k for k, (_, oa, ob, _) in enumerate(self.plan)}
        self.copies = []

    def at(self, oa, ob):
        origin = shifted(shifted(self.me, self.dims[0], -oa), self.dims[1], -ob)
        return self.place(index_in(origin, self.dims))

    def step(self, event):
        _, oa, ob, sends = event
        place = self.at(oa, ob)
        source = place
        if (oa, ob) == (0, 0):
            source = self.source
        else:
            slot = self.slots[oa, ob]
            near = shifted(self.me, self.dims[0], 1)
            remote(place, place, self.send_sem.at[0], self.recv_sem.at[slot], near).wait_recv()
        for to in sends:
            there = shifted(shifted(self.me, self.dims[0], to[0] - oa), self.dims[1], to[1] - ob)
            slot = self.slots[to]
            copy = remote(source, place, self.send_sem.at[slot], self.recv_sem.at[slot], there)
            copy.start()
            self.copies.append(copy)
        if (oa, ob) == (0, 0):
            self.own = pltpu.make_async_copy(source, place, self.own_sem)
            self.own.start()

    def finish(self):
        for copy in self.copies:
            copy.wait_send()


def run(*gathers):
    todo = [(e[0], n, e) for n, g in enumerate(gathers) for e in g.plan]
    for _, n, event in sorted(todo, key=lambda e: e[:2]):
        gathers[n].step(event)
    for g in gathers:
        g.own.wait()


def dot_f32(a, b):
    return jnp.dot(a, b, preferred_element_type=jnp.float32)


def split_three(x):
    high = x.astype(jnp.bfloat16)
    rest = x - high.astype(jnp.float32)
    middle = rest.astype(jnp.bfloat16)
    low = (rest - middle.astype(jnp.float32)).astype(jnp.bfloat16)
    return high, middle, low


def attend(scalars, q_ref, new_ref, cache_ref, left_ref, right_ref, queries, scores, weights):
    lengths, factor = scalars
    rows = q_ref.shape[0]
    scale = HEAD ** (-0.5)
    queries[...] = jnp.zeros_like(queries)
    for g in range(GROUP):
        queries[:, g, :] = q_ref[:, g * HEAD : (g + 1) * HEAD].astype(jnp.float32)
    lane = lax.broadcasted_iota(jnp.int32, (8, CACHE), 1)

    def along(j, r):
        row = jnp.full((8, CACHE), factor(j, 3, r))
        for b in (2, 1, 0):
            row = jnp.where(lane < (b + 1) * BLOCK_LEN, factor(j, b, r), row)
        return row

    for r in range(rows):
        raw = lax.dot_general(
            queries[r].astype(jnp.bfloat16),
            cache_ref[r, 0],
            (((1,), (1,)), ((), ())),
            preferred_element_type=jnp.float32,
        )
        scores[r] = jnp.where(lane < lengths[r], raw * along(0, r) * scale, -jnp.inf)
        weights[r] = along(1, r)
    fresh = new_ref[...].astype(jnp.float32)
    own = jnp.sum(queries[...] * fresh[:, 0:1, :], axis=2, keepdims=True) * scale
    s = scores[...]
    top = jnp.maximum(jnp.max(s, axis=2, keepdims=True), own)
    s = jnp.exp(s - top)
    own = jnp.exp(own - top)
    total = jnp.sum(s, axis=2, keepdims=True) + own
    weights[...] = s / total * weights[...]
    own = (own / total).astype(jnp.bfloat16).astype(jnp.float32) * fresh[:, 1:2, :]
    for r in range(rows):
        scores[r] = dot_f32(weights[r].astype(jnp.bfloat16), cache_ref[r, 1])
    scores[...] = scores[...] + own
    for g in range(GROUP):
        ref = left_ref if g < GROUP // 2 else right_ref
        at = g % (GROUP // 2)
        ref[:, at * HEAD : (at + 1) * HEAD] = scores[:, g, :].astype(ref.dtype)


def hand_off(cache_ref, factor, request, blocks, going_ref):
    for j in range(2):
        for b in range(CACHE // BLOCK_LEN):
            span = pl.ds(b * BLOCK_LEN, BLOCK_LEN)
            levels = cache_ref[request, j, span, :].astype(jnp.float32)
            going_ref[j, span, :] = jnp.where(
                b < blocks, levels * factor(j, b, request), 0.0
            ).astype(going_ref.dtype)


def route(choice_ref, slot_ref, pick_ref, expert):
    tokens = choice_ref.shape[1]
    experts = slot_ref.shape[0]
    ids = lax.broadcasted_iota(jnp.int32, (experts, tokens), 0)
    order = lax.broadcasted_iota(jnp.int32, (experts, tokens), 1)
    named = (choice_ref[0:1, :] == ids) | (choice_ref[1:2, :] == ids)
    count = named.astype(jnp.int32)
    step = 1
    while step < tokens:
        count = count + jnp.where(order >= step, pltpu.roll(count, step, 1), 0)
        step *= 2
    slots = jnp.where(named, count - 1, -1)
    slot_ref[...] = slots
    mine = jnp.sum(jnp.where(ids == expert, slots, 0).astype(jnp.float32).T, axis=1, keepdims=True)
    capacity = pick_ref.shape[1]
    across = lax.broadcasted_iota(jnp.int32, (tokens, capacity), 1).astype(jnp.float32)
    pick_ref[...] = (mine == across).astype(jnp.float32).astype(pick_ref.dtype)


def front_items():
    zy, yz, xc = ("z", "y"), ("y", "z"), ("x", "c")
    two, ring = ("two", "two"), ("ring", "ring")
    return {
        "left": (zy, two, 0),
        "right": (yz, two, 1),
        **{"part%d" % n: (xc, ring, n) for n in range(4)},
        "going0": (zy, ring, 0),
        "going1": (yz, ring, 1),
        **{"rows%d" % n: (zy if n % 2 == 0 else yz, ring, n // 2 + n % 2) for n in range(4)},
        "extra": (yz, ring, 0),
    }


PIECES = ((0, 64), (64, 32), (96, 48), (144, 48))
PARTS = ((0, 48), (48, 48), (96, 48), (144, 48))


def members(item):
    return SIZES[item[0][0]] * SIZES[item[0][1]]


def front_body(*refs):
    hbm, outs, scratch = refs[:13], refs[13:18], refs[18:]
    u_ref, factor_ref, hidden_ref, came_ref, slot_ref = outs
    local_refs, scratch = scratch[:13], scratch[13:]
    (
        lengths,
        precision,
        scales,
        mig_req,
        mig_blocks,
        q_ref,
        new_ref,
        cache_ref,
        choice_ref,
        w_ref,
        stream_ref,
        gain_ref,
        router_ref,
    ) = local_refs
    (
        left_ref,
        right_ref,
        going_ref,
        pick_ref,
        queries,
        scores,
        weights,
        left_all,
        right_all,
        part_own,
        part_all,
        rows_own,
        extra_own,
        extra_all,
        send_sem,
        recv_sem,
        own_sem,
        load_sem,
    ) = scratch
    me = coords()
    items = front_items()
    greeted = {}
    for dims, kinds, _ in items.values():
        for dim, steps in partners(dims, kinds).items():
            greeted.setdefault(dim, set()).update(steps)
    entered = greet(me, greeted)
    loads = [
        pltpu.make_async_copy(a, b, load_sem.at[k])
        for k, (a, b) in enumerate(zip(hbm, local_refs))
    ]
    for load in loads:
        load.start()

    def factor(j, b, r):
        return jnp.where(precision[b, r] == 1, scales[4 * j + b, r], 1.0)

    for load in loads[:8]:
        load.wait()
    attend(
        (lengths, factor), q_ref, new_ref, cache_ref, left_ref, right_ref, queries, scores, weights
    )
    rep = lax.axis_index("rep")
    entered()
    refs = {
        "left": (left_ref, lambda i: left_all.at[i]),
        "right": (right_ref, lambda i: right_all.at[i]),
        **{
            "part%d" % n: (
                part_own.at[pl.ds(*piece)],
                lambda i, piece=piece: part_all.at[i, pl.ds(*piece)],
            )
            for n, piece in enumerate(PARTS)
        },
        "going0": (going_ref.at[0], lambda i: came_ref.at[i, 0]),
        "going1": (going_ref.at[1], lambda i: came_ref.at[i, 1]),
        **{
            "rows%d" % n: (
                rows_own.at[pl.ds(*piece)],
                lambda i, piece=piece: u_ref.at[i, pl.ds(*piece)],
            )
            for n, piece in enumerate(PIECES)
        },
        "extra": (extra_own, lambda i: extra_all.at[i]),
    }
    g, base = {}, 0
    for n, (name, (dims, kinds, flip)) in enumerate(items.items()):
        sems = (send_sem, recv_sem, own_sem.at[n])
        g[name] = Gather(me, *refs[name], dims, kinds, flip, sems, base)
        base += members(items[name])
    moving = sorted(
        [(e[0], n, e) for n in (0, 1) for e in g["going%d" % n].plan], key=lambda e: e[:2]
    )

    def move(depth):
        while moving and moving[0][0] <= depth:
            _, n, event = moving.pop(0)
            g["going%d" % n].step(event)

    todo = sorted(
        [(e[0], n, e) for n, k in enumerate(("left", "right")) for e in g[k].plan],
        key=lambda e: e[:2],
    )
    for k, (cost, n, event) in enumerate(todo):
        if k == 2:
            hand_off(cache_ref, factor, mig_req[rep], mig_blocks[rep], going_ref)
            move(0)
            for load in loads[8:]:
                load.wait()
            route(choice_ref, slot_ref, pick_ref, lax.axis_index("hx"))
        g[("left", "right")[n]].step(event)
    for k in ("left", "right"):
        g[k].own.wait()

    split = left_ref.shape[1]
    tokens = stream_ref.shape[1]
    transposed = (((1,), (1,)), ((), ()))
    half = stream_ref.shape[0] // 2
    for n in range(2):
        span = pl.ds(n * half, half)
        part = lax.dot_general(
            w_ref[span, :split],
            left_all[...].reshape(tokens, split),
            transposed,
            preferred_element_type=jnp.float32,
        ) + lax.dot_general(
            w_ref[span, split:],
            right_all[...].reshape(tokens, split),
            transposed,
            preferred_element_type=jnp.float32,
        )
        part_own[span, :] = part.astype(part_own.dtype)
        for k in (2 * n, 2 * n + 1):
            g["part%d" % k].step(g["part%d" % k].plan.pop(0))
    move(4)

    def early(n):
        names = ["part%d" % k for k in (2 * n, 2 * n + 1)]
        found = sorted([(e[0], k, e) for k in names for e in g[k].plan], key=lambda e: e[:2])
        for _, k, event in found:
            g[k].step(event)
        for k in names:
            g[k].own.wait()
        move(8)

    gain = jnp.broadcast_to(gain_ref[...], (8, gain_ref.shape[1])).T[:, :1]
    squares = jnp.zeros((1, tokens), jnp.float32)
    logits = jnp.zeros((router_ref.shape[0], tokens), jnp.float32)
    for n in range(2):
        span = pl.ds(n * half, half)
        early(n)
        hidden = stream_ref[span, :].astype(jnp.float32)
        for e in range(part_all.shape[0]):
            hidden = hidden + part_all[e, span, :].astype(jnp.float32)
        hidden_ref[span, :] = hidden
        gained = hidden * gain[n * half : (n + 1) * half]
        rows_own[span, :] = dot_f32(gained.astype(jnp.bfloat16), pick_ref[...]).astype(
            rows_own.dtype
        )
        for k in (2 * n, 2 * n + 1):
            g["rows%d" % k].step(g["rows%d" % k].plan.pop(0))
        squares = squares + jnp.sum(hidden * hidden, axis=0, keepdims=True)
        logits = logits + jnp.dot(
            router_ref[:, n * half : (n + 1) * half].astype(jnp.float32),
            gained,
            precision=lax.Precision.HIGHEST,
            preferred_element_type=jnp.float32,
        )
    ids = lax.broadcasted_iota(jnp.int32, logits.shape, 0)
    choice = choice_ref[...]
    first = jnp.sum(jnp.where(choice[0:1] == ids, logits, 0.0), axis=0, keepdims=True)
    second = jnp.sum(jnp.where(choice[1:2] == ids, logits, 0.0), axis=0, keepdims=True)
    ahead = jnp.where(choice[0:1] == lax.axis_index("hx"), first - second, second - first)
    terms = jnp.concatenate(
        [t.astype(jnp.float32) for t in split_three(squares) + split_three(ahead)]
        + [jnp.zeros((2, tokens), jnp.float32)],
        axis=0,
    ).astype(jnp.bfloat16)
    chosen = dot_f32(terms, pick_ref[...])
    extra_own[...] = jnp.concatenate(
        [
            chosen[0:1] + chosen[1:2] + chosen[2:3],
            chosen[3:4] + chosen[4:5] + chosen[5:6],
            chosen[2:8] * 0.0,
        ],
        axis=0,
    )
    move(11)
    last = ("rows0", "rows1", "rows2", "rows3", "extra")
    todo = sorted(
        [(e[0], n, e) for n, k in enumerate(last) for e in g[k].plan],
        key=lambda e: e[:2],
    )
    for cost, n, event in todo:
        if cost > 8:
            move(cost - 2)
        g[last[n]].step(event)
    move(10**6)
    for k in (*last, "going0", "going1"):
        g[k].own.wait()
    sums = jnp.sum(extra_all[...], axis=0)
    inverse = lax.rsqrt(sums[0:1] / D + EPSILON)
    gate = 1.0 / (1.0 + jnp.exp(-sums[1:2] * inverse))
    factor_ref[...] = jnp.concatenate([inverse, gate, sums[2:8] * 0.0], axis=0)
    for k in g:
        g[k].finish()


def front(inputs, capacity, collective_id):
    query, stream = inputs[5], inputs[10]
    rows, wide = query.shape
    split = wide // 2
    mine, tokens = stream.shape
    half = mine // 2
    kind = query.dtype
    going = inputs[7].shape[1:]
    vmem = pl.BlockSpec(memory_space=pltpu.VMEM)
    anywhere = pl.BlockSpec(memory_space=pl.ANY)
    items = front_items()
    total = sum(members(item) for item in items.values())
    spaces = [pltpu.SMEM] * 5 + [pltpu.VMEM] * 8
    return pl.pallas_call(
        front_body,
        out_shape=[
            jax.ShapeDtypeStruct((32, mine, capacity), kind),
            jax.ShapeDtypeStruct((8, capacity), jnp.float32),
            jax.ShapeDtypeStruct((mine, tokens), jnp.float32),
            jax.ShapeDtypeStruct((32, *going), kind),
            jax.ShapeDtypeStruct((8, tokens), jnp.int32),
        ],
        in_specs=[pl.BlockSpec(memory_space=pltpu.HBM)] * 13,
        out_specs=[anywhere, vmem, vmem, anywhere, vmem],
        scratch_shapes=[space(x.shape, x.dtype) for space, x in zip(spaces, inputs)]
        + [
            pltpu.VMEM((rows, split), kind),
            pltpu.VMEM((rows, split), kind),
            pltpu.VMEM(going, kind),
            pltpu.VMEM((tokens, capacity), kind),
            pltpu.VMEM((rows, 8, HEAD), jnp.float32),
            pltpu.VMEM((rows, 8, HEAD), jnp.float32),
            pltpu.VMEM((rows, 8, HEAD), jnp.float32),
            pltpu.VMEM((32, rows, split), kind),
            pltpu.VMEM((32, rows, split), kind),
            pltpu.VMEM((mine, tokens), kind),
            pltpu.VMEM((8, mine, tokens), kind),
            pltpu.VMEM((mine, capacity), kind),
            pltpu.VMEM((8, capacity), jnp.float32),
            pltpu.VMEM((32, 8, capacity), jnp.float32),
            pltpu.SemaphoreType.DMA((total,)),
            pltpu.SemaphoreType.DMA((total,)),
            pltpu.SemaphoreType.DMA((len(items),)),
            pltpu.SemaphoreType.DMA((13,)),
        ],
        compiler_params=pltpu.CompilerParams(
            collective_id=collective_id, has_side_effects=True, vmem_limit_bytes=62 * 2**20
        ),
        name="front",
    )(*inputs)


SPANS = ((0, 256), (256, 128))


def down_body(
    raw_ref,
    w_hbm,
    factor_ref,
    hidden_hbm,
    slot_ref,
    came_hbm,
    dest_hbm,
    o_ref,
    arrived_ref,
    w_ref,
    hidden_ref,
    came_ref,
    dest_ref,
    act_ref,
    p2,
    p1,
    pm,
    r1,
    fin,
    place,
    *rest,
):
    s1_send, s1_recv, s2_send, s2_recv, z_send, z_recv, x_send, x_recv, x_own, load_sem = rest[10:]
    turned, tf, zr, out_own, out_all = (rest[2 * k : 2 * k + 2] for k in range(5))
    me = coords()
    xc, routes = ("x", "c"), (("two", "ring"), ("two", "ring"))
    entered = greet(me, {"y": {1, 3}, "z": set(range(1, 8)), **partners(xc, routes[1])})
    group = w_ref.shape[1] // 4
    loads = {}
    for k, step in enumerate((2, 1, 3, 0)):
        start = pl.multiple_of(lax.rem(me["y"] + step, 4) * group, 128)
        span = pl.ds(start, group)
        loads[step] = pltpu.make_async_copy(w_hbm.at[:, span], w_ref.at[:, span], load_sem.at[k])
        loads[step].start()
    late = [
        pltpu.make_async_copy(a, b, load_sem.at[4 + k])
        for k, (a, b) in enumerate(
            ((hidden_hbm, hidden_ref), (came_hbm, came_ref), (dest_hbm, dest_ref))
        )
    ]
    up, down = shifted(me, "y", 1), shifted(me, "y", -1)
    pair, odd = me["z"] // 2, lax.rem(me["z"], 2)
    wide = w_ref.shape[1] // 16
    n = wide // 4
    order = (2, 1, 3, 0)
    tokens = slot_ref.shape[1]
    copies, firsts, lasts, across = [], {}, {}, {}

    def product(p, step, k):
        there = lax.rem(me["y"] + step, 4)
        start = there * (4 * wide) + lax.rem(pair + k, 4) * wide
        rows = act_ref[pl.ds(*SPANS[p]), :]
        return dot_f32(rows, w_ref[:, pl.ds(pl.multiple_of(start, 128), wide)])

    def send(source, place, ss, rs, there):
        copy = remote(source, place, ss, rs, there)
        copy.start()
        copies.append(copy)
        return copy

    def halves(p):
        first, size = SPANS[p]
        return pl.ds(first, size // 2), pl.ds(first + size // 2, size // 2)

    def begin(p, k):
        low, high = halves(p)
        p2[k, pl.ds(*SPANS[p])] = product(p, 2, k).astype(p2.dtype)
        if (p, k) == (0, order[0]):
            entered()
        firsts[p, k] = (
            send(p2.at[k, low], r1.at[k, low], s1_send.at[p, k, 0], s1_recv.at[p, k, 0], up),
            send(p2.at[k, high], r1.at[k, high], s1_send.at[p, k, 1], s1_recv.at[p, k, 1], down),
        )

    def middle(p, k):
        low, high = halves(p)

        def on(source, side, piece, there):
            at = (p, k, side, 0 if piece is low else 1)
            return send(
                source.at[k, piece], fin.at[k, side, piece], s2_send.at[at], s2_recv.at[at], there
            )

        p1[k, pl.ds(*SPANS[p])] = product(p, 1, k).astype(p1.dtype)
        c = on(p1, 0, high, up)
        pm[k, pl.ds(*SPANS[p])] = product(p, 3, k).astype(pm.dtype)
        d = on(pm, 1, low, down)
        firsts[p, k][0].wait_recv()
        p1[k, low] = (p1[k, low].astype(jnp.float32) + r1[k, low].astype(jnp.float32)).astype(
            p1.dtype
        )
        e = on(p1, 0, low, up)
        firsts[p, k][1].wait_recv()
        pm[k, high] = (pm[k, high].astype(jnp.float32) + r1[k, high].astype(jnp.float32)).astype(
            pm.dtype
        )
        lasts[p, k] = (c, d, e, on(pm, 1, high, down))

    def end(p, k):
        whole = product(p, 0, k)
        for copy in lasts[p, k]:
            copy.wait_recv()
        span = pl.ds(*SPANS[p])
        whole = whole + (fin[k, 0, span].astype(jnp.float32) + fin[k, 1, span].astype(jnp.float32))
        whole = whole.T
        for e in range(2):
            part = whole[e * (wide // 2) : (e + 1) * (wide // 2)]
            turned[p][k, e] = part.astype(turned[p].dtype)
            if k == 0:
                tf[p][e] = part
        first = 2 * lax.rem(pair + k, 4)
        if k > 0:
            for e in range(2):
                slot = 2 * k + odd
                send(
                    turned[p].at[k, e],
                    zr[p].at[slot],
                    z_send.at[p, 2 * k + e],
                    z_recv.at[p, slot],
                    dict(me, z=first + e),
                )
        else:
            send(
                turned[p].at[0, 1 - odd],
                zr[p].at[odd],
                z_send.at[p, 0],
                z_recv.at[p, odd],
                dict(me, z=first + 1 - odd),
            )

    def total(p):
        found = tf[p][odd]
        for k in order:
            for e in range(2) if k > 0 else (0,):
                slot = 2 * k + e if k > 0 else 1 - odd
                remote(
                    zr[p].at[slot], zr[p].at[slot], z_send.at[p, 0], z_recv.at[p, slot], up
                ).wait_recv()
                found = found + zr[p][slot].astype(jnp.float32)
        found = found * factor_ref[1:2, pl.ds(*SPANS[p])]
        for h in range(2):
            out_own[p][h] = found[h * n : (h + 1) * n].astype(out_own[p].dtype)
            gather = Gather(
                me,
                out_own[p].at[h],
                lambda i, h=h: out_all[p].at[i, h],
                xc,
                routes[p],
                h,
                (x_send, x_recv, x_own.at[2 * p + h]),
                8 * (2 * p + h),
            )
            gather.step(gather.plan.pop(0))
            across[p, h] = gather

    def one_hot(p):
        first, size = SPANS[p]
        slots = lax.broadcasted_iota(jnp.int32, (size, tokens), 0) + first
        for e in range(8):
            place[e, pl.ds(first, size)] = (
                (slot_ref[e : e + 1, :] == slots).astype(jnp.float32).astype(place.dtype)
            )

    def combine(p):
        run(across[p, 0], across[p, 1])
        for h in range(2):
            span = pl.ds(h * n, n)
            mixed = hidden_ref[span, :]
            for e in range(8):
                mixed = mixed + dot_f32(out_all[p][e, h], place[e, pl.ds(*SPANS[p])])
            hidden_ref[span, :] = mixed

    inverse = jnp.broadcast_to(factor_ref[0:1, :], factor_ref.shape).T[:, :1]
    depth = act_ref.shape[1]
    gate = raw_ref[:, :depth] * inverse
    act = gate * (1.0 / (1.0 + jnp.exp(-gate))) * (raw_ref[:, depth:] * inverse)
    act_ref[...] = act.astype(act_ref.dtype)
    loads[2].wait()
    for k in order:
        begin(0, k)
    loads[1].wait()
    loads[3].wait()
    for load in late:
        load.start()
    for k in order:
        middle(0, k)
    for k in order:
        begin(1, k)
    loads[0].wait()
    end(0, 2)
    end(0, 1)
    one_hot(0)
    one_hot(1)
    end(0, 3)
    middle(1, 2)
    end(0, 0)
    for k in (1, 3, 0):
        middle(1, k)
    for load in late:
        load.wait()
    rep = lax.axis_index("rep")
    n_rep = dest_ref.shape[0]
    first, last = jnp.int32(n_rep), jnp.int32(-1)
    for source in range(n_rep):
        aimed = dest_ref[source] == rep
        first = jnp.where(aimed, jnp.minimum(first, source), first)
        last = jnp.where(aimed, source, last)
    for q, (source, there) in enumerate(((first, last >= 0), (last, last > first))):
        block = came_ref[jnp.clip(source, 0, n_rep - 1)].astype(jnp.float32)
        arrived_ref[0, q] = jnp.where(there, block, 0.0).astype(arrived_ref.dtype)
    end(1, 2)
    end(1, 1)
    total(0)
    end(1, 3)
    end(1, 0)
    combine(0)
    total(1)
    combine(1)
    o_ref[...] = hidden_ref[...].astype(o_ref.dtype)
    for copy in copies:
        copy.wait_send()
    for gather in across.values():
        gather.finish()


def down_and_scatter(raw, w_down, factors, hidden, slots, came, mig_dest, collective_id):
    rows, depth = raw.shape[0], w_down.shape[0]
    width = w_down.shape[1] // 16
    vmem = pl.BlockSpec(memory_space=pltpu.VMEM)
    hbm = pl.BlockSpec(memory_space=pltpu.HBM)
    kind = w_down.dtype
    return pl.pallas_call(
        down_body,
        out_shape=[
            jax.ShapeDtypeStruct(hidden.shape, kind),
            jax.ShapeDtypeStruct((1, IN_MOST, *came.shape[1:]), kind),
        ],
        in_specs=[vmem, hbm, vmem, hbm, vmem, hbm, hbm],
        out_specs=[vmem, vmem],
        scratch_shapes=[
            pltpu.VMEM(w_down.shape, kind),
            pltpu.VMEM(hidden.shape, hidden.dtype),
            pltpu.VMEM(came.shape, kind),
            pltpu.SMEM(mig_dest.shape, mig_dest.dtype),
            pltpu.VMEM((rows, depth), kind),
            pltpu.VMEM((4, rows, width), kind),
            pltpu.VMEM((4, rows, width), kind),
            pltpu.VMEM((4, rows, width), kind),
            pltpu.VMEM((4, rows, width), kind),
            pltpu.VMEM((4, 2, rows, width), kind),
            pltpu.VMEM((8, rows, slots.shape[1]), kind),
            *[pltpu.VMEM((4, 2, width // 2, size), kind) for _, size in SPANS],
            *[pltpu.VMEM((2, width // 2, size), jnp.float32) for _, size in SPANS],
            *[pltpu.VMEM((8, width // 2, size), kind) for _, size in SPANS],
            *[pltpu.VMEM((2, width // 4, size), kind) for _, size in SPANS],
            *[pltpu.VMEM((8, 2, width // 4, size), kind) for _, size in SPANS],
            pltpu.SemaphoreType.DMA((2, 4, 2)),
            pltpu.SemaphoreType.DMA((2, 4, 2)),
            pltpu.SemaphoreType.DMA((2, 4, 2, 2)),
            pltpu.SemaphoreType.DMA((2, 4, 2, 2)),
            pltpu.SemaphoreType.DMA((2, 8)),
            pltpu.SemaphoreType.DMA((2, 8)),
            pltpu.SemaphoreType.DMA((32,)),
            pltpu.SemaphoreType.DMA((32,)),
            pltpu.SemaphoreType.DMA((4,)),
            pltpu.SemaphoreType.DMA((7,)),
        ],
        compiler_params=pltpu.CompilerParams(
            collective_id=collective_id, has_side_effects=True, vmem_limit_bytes=62 * 2**20
        ),
        name="down_scatter",
    )(raw, w_down, factors, hidden, slots, came, mig_dest)


def finish_body(mixed_ref, arrived_ref, mixed_out, arrived_out):
    mixed_out[...] = mixed_ref[...]
    arrived_out[...] = arrived_ref[...]


def finish(mixed, arrived):
    vmem = pl.BlockSpec(memory_space=pltpu.VMEM)
    return pl.pallas_call(
        finish_body,
        out_shape=[jax.ShapeDtypeStruct(x.shape, x.dtype) for x in (mixed, arrived)],
        in_specs=[vmem] * 2,
        out_specs=[vmem] * 2,
        name="finish",
    )(mixed, arrived)


def contract_first(a, b, **kw):
    return lax.dot_general(
        a, b, (((0,), (0,)), ((), ())), preferred_element_type=jnp.float32, **kw
    )


def local(
    stream_in,
    query,
    new_kv,
    cache,
    precision,
    cache_scale,
    lengths,
    w_heads,
    norm_gain,
    w_router,
    expert_choice,
    w_in,
    w_down,
    mig_dest,
    mig_req,
    mig_blocks,
):
    tokens = stream_in.shape[0]
    capacity = tokens // 2
    ff = w_in.shape[3]
    choice = expert_choice.T
    rows = query.shape[0]
    u_all, factors, hidden, came, slots = front(
        [
            lengths,
            precision.T,
            jnp.transpose(cache_scale[..., 0], (1, 2, 0)).reshape(-1, rows),
            mig_req,
            mig_blocks,
            query,
            new_kv,
            cache,
            choice,
            w_heads.T,
            stream_in.T,
            norm_gain[None],
            w_router.T,
        ],
        capacity,
        1,
    )
    w_in, u_all = lax.optimization_barrier((w_in, u_all))
    gate_up = contract_first(u_all.reshape(D, capacity), w_in[0].reshape(D, 2 * ff))
    mixed, arrived = down_and_scatter(
        gate_up, w_down[0], factors, hidden, slots, came, mig_dest, 2
    )
    mixed, arrived = finish(mixed, arrived)
    return (mixed.T, arrived)


def solution(mesh):
    placed = (
        P(None, "rep"),
        P("rep", "hx"),
        P("rep", None, "hx"),
        P("rep", None, None, "hx"),
        P("rep", None),
        P("rep", None, None, "hx"),
        P("rep"),
        P("hx", "rep"),
        P("rep"),
        P("rep", None),
        P(),
        P("hx", None, None, "rep"),
        P("hx", "rep", None),
        P(),
        P(),
        P(),
    )
    return jax.shard_map(
        local,
        mesh=mesh,
        in_specs=placed,
        out_specs=(P(None, "rep"), P("rep", None, None, None, "hx")),
        check_vma=False,
    )
```
